256 devices in a mesh: fsdp: 16 (over z_hi, x), tensor: 4 (over z_lo, core), replica: 4 (over y).
Axes of the slice: x: 4, y: 4, z: 8 (z_hi: 4, z_lo: 2; z = z_hi * 2 + z_lo), core: 2. Of those that a mesh axis runs over, the one named last changes fastest.
Arguments:
- activations: bfloat16 [24576, 8192], P(('fsdp', 'replica'))
- norm_gain: float32 [8192], replicated, may hold values from 0.1 to 1.9
- key_weight: bfloat16 [8192, 1024], P('fsdp', 'tensor'), may hold values from -0.0625 to 0.0625
- value_weight: bfloat16 [8192, 1024], P('fsdp', 'tensor'), may hold values from -0.0625 to 0.0625
- key_cot: bfloat16 [24576, 1024], P(('fsdp', 'replica'), 'tensor'), may hold values from -6 to 6
- value_cot: bfloat16 [24576, 1024], P(('fsdp', 'replica'), 'tensor'), may hold values from -6 to 6
- blocks: int32 [2, 64, 2], P(None, 'tensor'), may hold values from 0 to 127, as said below
Outputs:
- key_out: bfloat16 [24576, 1024], P(('fsdp', 'replica'), 'tensor')
- value_out: bfloat16 [24576, 1024], P(('fsdp', 'replica'), 'tensor')
- normed_grad: bfloat16 [24576, 8192], P(('fsdp', 'replica'), 'tensor')
- block_grads: float32 [2, 64, 4096], P(None, 'tensor')
The draws below stay inside these ranges and needn't reach their ends.
Inputs may be any that keep to these rules, and one draw needn't show every extreme that they name: Each run of 16 entries of one projection names 16 distinct blocks of one tensor shard, as (row block below 128, column block below the shard's key columns / 64).
All inputs are finite; a program needn't handle non-finite values.
Results may differ from the reference program's by a relative error of at most 0.013.
Values may be sent and summed in bfloat16 or wider, within the bound.
A program may use at most 128 MiB of HBM per device.

```python
import math
import jax
import jax.numpy as jnp
from jax import lax

D = 8192
KVW = 1024
BLK = 64
NB = 16
TOKENS = 24576
NBT = 64
N_TENSOR = 4


def draw_activations(key, part):
    row_key = jax.random.fold_in(key, 11)
    column_key = jax.random.fold_in(key, 12)
    base_key = jax.random.fold_in(key, 13)
    row_scale = jnp.exp(jax.random.uniform(row_key, (TOKENS, 1), jnp.float32) * math.log(10.0))
    column_scale = jnp.exp(jax.random.uniform(column_key, (1, D), jnp.float32) * math.log(10.0))
    values = jax.random.normal(base_key, (TOKENS, D), jnp.float32)
    return (values * row_scale * column_scale).astype(jnp.bfloat16)


def draw_blocks(key, part):
    width_blocks = KVW // N_TENSOR // BLK
    per_shard = D // BLK * width_blocks
    last_block = (D // BLK - 1) * width_blocks

    def choose_shard(number):
        shard_key = jax.random.fold_in(key, number)
        others = jax.random.permutation(shard_key, per_shard - width_blocks)[:NB - 1]
        picked = jnp.concatenate([others, jnp.full((1,), last_block, jnp.int32)])
        order = jax.random.permutation(jax.random.fold_in(shard_key, 7), NB)
        picked = picked[order]
        return jnp.stack([picked // width_blocks, picked % width_blocks], axis=-1)
    coords_table = jax.vmap(choose_shard)(jnp.arange(2 * N_TENSOR, dtype=jnp.int32))
    return coords_table.reshape(2, N_TENSOR * NB, 2).astype(jnp.int32)


def shard_levels(own_key, dims, shards, low, largest):
    factor_of, own = 1.0, jax.random.fold_in(own_key, 6)
    for position, blocks in shards:
        steps = jnp.exp(jax.random.uniform(jax.random.fold_in(own, position), (blocks,), jnp.float32, low / len(shards), largest / len(shards)))
        factor_of = factor_of * jnp.repeat(steps, dims[position] // blocks).reshape([-1 if axis == position else 1 for axis in range(len(dims))])
    return factor_of


def scatter_about(rng, dims, deviation, limit, split=(), kind=jnp.bfloat16):
    factor_of = shard_levels(rng, dims, split, -0.22, 0.18) if split else 1.0
    drawn = jax.random.normal(rng, dims, jnp.float32) * deviation * factor_of
    return jnp.minimum(jnp.maximum(drawn, -limit), limit).astype(kind)


def setup_inputs(seed: int = 0) -> dict:
    streams_of = jax.random.split(jax.random.key(seed), 8)
    return {
        "activations": draw_activations(jax.random.fold_in(streams_of[7], 71), 0),
        "norm_gain": jnp.clip(1.0 + 0.18 * jax.random.normal(streams_of[1], (D,), jnp.float32), 0.1, 1.9),
        "key_weight": scatter_about(streams_of[2], (D, KVW), D ** -0.5, 0.0625, ((0, 16), (1, 4))),
        "value_weight": scatter_about(streams_of[3], (D, KVW), D ** -0.5, 0.0625, ((0, 16), (1, 4))),
        "key_cot": scatter_about(streams_of[4], (TOKENS, KVW), 1.0, 6.0, ((0, 64), (1, 4))),
        "value_cot": scatter_about(streams_of[5], (TOKENS, KVW), 1.0, 6.0, ((0, 64), (1, 4))),
        "blocks": draw_blocks(jax.random.fold_in(streams_of[7], 71), 0),
    }


norm_epsilon = 1e-05

def block_product(normed, cotangent, coords):
    shard_width = KVW // N_TENSOR

    def single(entries):
        number, row_block, column_block = entries
        shard_number = number // NB
        left_block = lax.dynamic_slice_in_dim(normed, (row_block * BLK).astype(jnp.int32), BLK, 1)
        first_col = (shard_number * shard_width + column_block * BLK).astype(jnp.int32)
        right_block = lax.dynamic_slice_in_dim(cotangent, first_col, BLK, 1)
        return jnp.dot(left_block.T, right_block, preferred_element_type=jnp.float32).reshape(BLK * BLK)
    numbers = jnp.arange(NBT, dtype=jnp.int32)
    return lax.map(single, (numbers, coords[:, 0].astype(jnp.int32), coords[:, 1].astype(jnp.int32)))

def reference(activations, norm_gain, key_weight, value_weight, key_cot, value_cot, blocks):
    widened = activations.astype(jnp.float32)
    inverse_rms = lax.rsqrt(lax.optimization_barrier(jnp.mean(widened * widened, axis=1, keepdims=True)) + norm_epsilon)
    normed = (widened * inverse_rms * norm_gain).astype(jnp.bfloat16)
    key_out = jnp.dot(normed, key_weight, preferred_element_type=jnp.float32).astype(jnp.bfloat16)
    value_out = jnp.dot(normed, value_weight, preferred_element_type=jnp.float32).astype(jnp.bfloat16)
    shard_width = KVW // N_TENSOR
    summed_total = jnp.zeros((TOKENS, D), jnp.float32)
    for shard_number in range(N_TENSOR):
        low_col = shard_number * shard_width
        high_col = low_col + shard_width
        partial_value = jnp.dot(key_cot[:, low_col:high_col], key_weight[:, low_col:high_col].T, preferred_element_type=jnp.float32)
        partial_value = partial_value + jnp.dot(value_cot[:, low_col:high_col], value_weight[:, low_col:high_col].T, preferred_element_type=jnp.float32)
        rounded = lax.optimization_barrier(partial_value.astype(jnp.bfloat16))
        summed_total = summed_total + rounded.astype(jnp.float32)
    normed_grad = summed_total.astype(jnp.bfloat16)
    block_grads = jnp.stack([block_product(normed, key_cot, blocks[0]), block_product(normed, value_cot, blocks[1])])
    return (key_out, value_out, normed_grad, block_grads)
```

```python
import functools

import jax
import jax.numpy as jnp
from jax import lax
from jax.experimental import pallas as pl
from jax.experimental.pallas import tpu as pltpu
from jax.sharding import PartitionSpec as P

D = 8192
TOK = 384
EPS = 1e-05
F32 = jnp.float32
BF16 = jnp.bfloat16
ROWS = 64
RA = 64

AXP, AXM, AXFP, AXFM, BYP, BYM, BYFP, BYFM, AYP, AYM, AYFP, AYFM, BXP, BXM, BXFP, BXFM = range(16)
OP0, OP1, OM0, OM1, OFP, OFM, ZP, ZM, ZFP, ZFM = range(10)


def body(
    act_hbm, gain_hbm, kw_hbm, vw_hbm, kc_hbm, vc_hbm, blocks,
    key_out, value_out, grad_out, bg_out,
    wbuf, act, normed, gain, cot, acc, pbuf, rbuf, qbuf,
    g32, s1, r1, p1, s2, r2, p2, s3, r3, tall,
    ld, xs, xr, os, orr, bs, br, ss, sr, qs, qr,
):
    f = lax.axis_index("fsdp")
    t = lax.axis_index("tensor")
    y = lax.axis_index("replica")
    zh, x = f // 4, f % 4
    zl = t // 2

    def m4(v):
        return lax.rem(v + 4, 4)

    def xdev(d):
        return {"fsdp": zh * 4 + m4(x + d)}

    def ydev(d):
        return {"replica": m4(y + d)}

    def zdev(d):
        return {"fsdp": m4(zh + d) * 4 + x}

    sib = {"tensor": t + 1 - 2 * (t % 2)}
    zpair = {"tensor": lax.rem(t + 2, 4)}

    loads = []

    def load(src, dst):
        c = pltpu.make_async_copy(src, dst, ld.at[len(loads)])
        c.start()
        loads.append(c)

    load(kw_hbm, wbuf.at[zh, x, :, :, pl.ds(0, 256)])
    load(vw_hbm, wbuf.at[zh, x, :, :, pl.ds(256, 256)])
    load(gain_hbm, gain)
    for i in range(4):
        load((kc_hbm, vc_hbm)[i // 2].at[:, pl.ds(i % 2 * 128, 128)], cot.at[i])
    for i in range(TOK // ROWS):
        load(act_hbm.at[pl.ds(i * ROWS, ROWS)], act.at[pl.ds(i * ROWS, ROWS)])

    barrier = pltpu.get_barrier_semaphore()
    peers = [xdev(1), xdev(-1), xdev(2), ydev(1), ydev(-1), ydev(2), zdev(1), zdev(-1), zdev(2), sib, zpair]
    for peer in peers:
        pl.semaphore_signal(barrier, inc=1, device_id=peer, device_id_type=pl.DeviceIdType.MESH)
    pl.semaphore_wait(barrier, len(peers))

    sent = []

    def rcopy(src, dst, a, b, dev):
        return pltpu.make_async_remote_copy(
            src_ref=src, dst_ref=dst, send_sem=a, recv_sem=b, device_id=dev,
            device_id_type=pl.DeviceIdType.MESH,
        )

    def piece(kind, zz, px, py):
        a, b = pl.ds(0, RA), pl.ds(RA, 128 - RA)
        if kind in (AXP, AXM):
            return wbuf.at[zz, px, py, a]
        if kind == AXFP:
            return wbuf.at[zz, m4(px - 1), py, pl.ds(0, RA // 2)]
        if kind == AXFM:
            return wbuf.at[zz, m4(px + 1), py, pl.ds(RA // 2, RA // 2)]
        if kind in (BYP, BYM):
            return wbuf.at[zz, px, py, b]
        if kind == BYFP:
            return wbuf.at[zz, px, m4(py - 1), pl.ds(RA, (128 - RA) // 2)]
        if kind == BYFM:
            return wbuf.at[zz, px, m4(py + 1), pl.ds(RA + (128 - RA) // 2, (128 - RA) // 2)]
        if kind in (AYP, AYM):
            return wbuf.at[zz, :, py, a]
        if kind == AYFP:
            return wbuf.at[zz, pl.ds(0, 2), m4(py - 1), a]
        if kind == AYFM:
            return wbuf.at[zz, pl.ds(2, 2), m4(py + 1), a]
        if kind in (BXP, BXM):
            return wbuf.at[zz, px, :, b]
        if kind == BXFP:
            return wbuf.at[zz, m4(px - 1), pl.ds(0, 2), b]
        return wbuf.at[zz, m4(px + 1), pl.ds(2, 2), b]

    along_x = (AXP, AXM, AXFP, AXFM, BXP, BXM, BXFP, BXFM)
    plus = (AXP, AXFP, BYP, BYFP, AYP, AYFP, BXP, BXFP)

    def xy(kind, zz, incoming):
        d = 1 if kind in plus else -1
        back = d if incoming else 0
        if kind in along_x:
            ref, dev = piece(kind, zz, m4(x - back), y), xdev(d)
        else:
            ref, dev = piece(kind, zz, x, m4(y - back)), ydev(d)
        return rcopy(ref, ref, xs.at[kind, zz], xr.at[kind, zz], dev)

    def send(zz, *kinds):
        for kind in kinds:
            c = xy(kind, zz, False)
            c.start()
            sent.append(c)

    def recv(zz, *kinds):
        for kind in kinds:
            xy(kind, zz, True).wait_recv()

    def own(kind, incoming):
        d = 1 if kind in (OP0, OP1, OFP, ZP, ZFP) else -1
        back = d if incoming else 0
        px, pz = m4(x - back), m4(zh - back)
        if kind in (OP0, OM0):
            ref = wbuf.at[zh, px, pl.ds(0, 2)]
        elif kind in (OP1, OM1):
            ref = wbuf.at[zh, px, pl.ds(2, 2)]
        elif kind == OFP:
            ref = wbuf.at[zh, m4(px - 1), pl.ds(0, 2)]
        elif kind == OFM:
            ref = wbuf.at[zh, m4(px + 1), pl.ds(2, 2)]
        elif kind in (ZP, ZM):
            ref = wbuf.at[pz, x, y]
        elif kind == ZFP:
            ref = wbuf.at[m4(pz - 1), x, y, pl.ds(0, 64)]
        else:
            ref = wbuf.at[m4(pz + 1), x, y, pl.ds(64, 64)]
        dev = zdev(d) if kind >= ZP else xdev(d)
        return rcopy(ref, ref, os.at[kind], orr.at[kind], dev)

    def osend(*kinds):
        for kind in kinds:
            c = own(kind, False)
            c.start()
            sent.append(c)

    def orecv(*kinds):
        for kind in kinds:
            own(kind, True).wait_recv()

    def norm_rows(i):
        loads[7 + i].wait()

        @pl.loop(0, ROWS // 16)
        def _(k):
            rows = pl.ds(pl.multiple_of(i * ROWS + k * 16, 16), 16)
            total = jnp.zeros((16, 128), F32)
            for j in range(D // 512):
                v = act[rows, pl.ds(j * 512, 512)].astype(F32)
                v = v * v
                total = total + ((v[:, 0:128] + v[:, 128:256]) + (v[:, 256:384] + v[:, 384:512]))
            inv = lax.rsqrt(jnp.sum(total, axis=1, keepdims=True) / D + EPS)
            for j in range(D // 128):
                cols = pl.ds(j * 128, 128)
                v = act[rows, cols].astype(F32)
                normed[j, rows] = (v * inv * gain[:, cols]).astype(BF16)

    def block_entry(p, n):
        row, column = blocks[p, n, 0], blocks[p, n, 1]
        row_odd, column_odd = lax.rem(row, 2), lax.rem(column, 2)
        left = normed[lax.div(row, 2)]
        right = cot[2 * p + lax.div(column, 2)]
        full = lax.dot_general(left, right, (((0,), (0,)), ((), ())), preferred_element_type=F32)
        low = row_odd.astype(F32)
        half = full[64:] * low + full[:64] * (1.0 - low)
        move = column_odd.astype(F32) if p == 0 else 1.0 - column_odd.astype(F32)
        return pltpu.roll(half, 64, 1) * move + half * (1.0 - move)

    lane = lax.broadcasted_iota(jnp.int32, (64, 128), 1)

    def block_products(lo, hi):
        @pl.loop(lo, hi)
        def _(n):
            value = jnp.where(lane < 64, block_entry(0, n), block_entry(1, n))
            g32[n // 4, n % 4] = value
            s1[n // 4, n % 4] = value.astype(BF16)

    def shard(zz, xx):
        w = wbuf[zz, xx].reshape(512, 512)
        tile = (zz * 4 + xx) * 4
        left = jnp.concatenate([normed[tile + j] for j in range(4)], axis=1)
        acc[...] += jnp.dot(left, w, preferred_element_type=F32)
        both = jnp.concatenate([cot[j] for j in range(4)], axis=1)
        part = lax.dot_general(both, w, (((1,), (1,)), ((), ())), preferred_element_type=F32)
        pbuf[zz, xx] = part.astype(BF16)
        odd = lax.rem(zz + t, 2) == 1

        @pl.when(odd)
        def _():
            sibcopy(zz, xx).start()

    def sibcopy(zz, xx):
        slot = (zz // 2 - zl) * (zz // 2 - zl)
        return rcopy(pbuf.at[zz, xx], rbuf.at[slot, xx], ss.at[slot * 4 + xx], sr.at[slot * 4 + xx], sib)

    def qcopy(zz, xx):
        return rcopy(pbuf.at[zz, xx], qbuf.at[xx], qs.at[xx], qr.at[xx], zpair)

    def rwait(slot, xx):
        rcopy(rbuf.at[slot, xx], rbuf.at[slot, xx], ss.at[slot * 4 + xx], sr.at[slot * 4 + xx], sib).wait_recv()

    away = lax.rem(t + 2, 4)

    def combine(zz, xx):
        @pl.when(zz == away)
        def _():
            rwait(1, xx)
            pbuf[zz, xx] = (pbuf[zz, xx].astype(F32) + rbuf[1, xx].astype(F32)).astype(BF16)
            qcopy(zz, xx).start()

    dist = (1, -1, 2)

    def bg_copy(stage, d, incoming):
        back = d if incoming else 0
        axis = (0, 1, 2, 2, 1, 0)[stage]
        me = (y, x, zh)[axis]
        dev = (ydev, xdev, zdev)[axis](d)
        sender = m4(me - back)
        target = m4(sender + d)
        if stage < 3:
            src, dst = (s1, s2, s3)[stage].at[target], (r1, r2, r3)[stage].at[sender]
        else:
            where = [y, x, zh]
            where[axis] = sender
            src = dst = tall.at[tuple(where[: axis + 1])]
        i = stage * 3 + dist.index(d)
        return rcopy(src, dst, bs.at[i], br.at[i], dev)

    def bg_send(stage):
        for d in dist:
            c = bg_copy(stage, d, False)
            c.start()
            sent.append(c)

    def bg_recv(stage):
        for d in dist:
            bg_copy(stage, d, True).wait_recv()

    def bg_sum(stage):
        bg_recv(stage)
        if stage == 0:
            total = g32[y]
            for d in dist:
                total = total + r1[m4(y - d)].astype(F32)
            p1[...] = total
            s2[...] = total.astype(BF16)
        elif stage == 1:
            total = p1[x]
            for d in dist:
                total = total + r2[m4(x - d)].astype(F32)
            total = total.reshape(4, 16, 128)
            p2[...] = total
            s3[...] = total.astype(BF16)
        else:
            total = p2[zh]
            for d in dist:
                total = total + r3[m4(zh - d)].astype(F32)
            tall[y, x, zh] = total.astype(BF16)
        bg_send(stage + 1)

    own_away = (zh // 2 - zl) * (zh // 2 - zl)
    other = zh + 1 - 2 * (zh % 2)
    first = own_away * other + (1 - own_away) * (2 - 2 * zl)
    second = own_away * (2 * zl) + (1 - own_away) * (3 - 2 * zl)
    third = own_away * (2 * zl + 1) + (1 - own_away) * other
    order = (first, second, third)

    def small(zz):
        send(zz, AXP, AXM, BYP, BYM)

    def small_forward(zz):
        recv(zz, AXP, BYP)
        send(zz, AXFP, BYFP)
        recv(zz, AXM, BYM)
        send(zz, AXFM, BYFM)

    def big(zz):
        recv(zz, AXFP, AXFM)
        send(zz, AYP, AYM)
        recv(zz, BYFP, BYFM)
        send(zz, BXP, BXM)

    def big_forward(zz):
        recv(zz, AYP, BXP)
        send(zz, AYFP, BXFP)
        recv(zz, AYM, BXM)
        send(zz, AYFM, BXFM)

    def big_end(zz):
        recv(zz, AYFP, AYFM, BXFP, BXFM)

    loads[0].wait()
    loads[1].wait()
    osend(ZP, ZM, OP0, OM1, OP1, OM0)
    acc[...] = jnp.zeros_like(acc)
    loads[2].wait()
    for i in range(TOK // ROWS):
        norm_rows(i)
    orecv(ZP, ZM)
    osend(ZFP, ZFM)
    small(m4(zh - 1))
    small(m4(zh + 1))
    for i in range(3, 7):
        loads[i].wait()
    orecv(OP0)
    osend(OFP)
    orecv(OM1)
    osend(OFM)
    orecv(ZFP, ZFM)
    small(m4(zh + 2))
    block_products(0, 16)
    bg_send(0)
    small_forward(first)
    small_forward(second)
    small_forward(third)
    shard(zh, x)
    big(first)
    combine(zh, x)
    orecv(OP1, OM0)
    bg_sum(0)
    shard(zh, m4(x + 1))
    big(second)
    shard(zh, m4(x - 1))
    combine(zh, m4(x + 1))
    bg_sum(1)
    big(third)
    orecv(OFP, OFM)
    shard(zh, m4(x + 2))
    combine(zh, m4(x - 1))
    bg_sum(2)
    combine(zh, m4(x + 2))
    for k, zz in enumerate(order):
        big_forward(zz)
        big_end(zz)
        if k == 0:
            bg_recv(3)
            bg_send(4)
        if k == 1:
            bg_recv(4)
            bg_send(5)
        for i in range(4):
            shard(zz, i)
            if i > 0:
                combine(zz, i - 1)
        combine(zz, 3)
    key_out[...] = acc[:, 0:256].astype(BF16)
    value_out[...] = acc[:, 256:512].astype(BF16)
    bg_recv(5)
    bg_out[...] = tall[...].astype(F32).reshape(16, 64, 128)
    for i in range(4):
        rwait(0, i)
        rcopy(qbuf.at[i], qbuf.at[i], qs.at[i], qr.at[i], zpair).wait_recv()
        total = pbuf[t, i].astype(F32) + rbuf[0, i].astype(F32) + qbuf[i].astype(F32)
        grad_out[:, pl.ds(i * 512, 512)] = total.astype(BF16)

    for c in sent:
        c.wait_send()
    for i in range(4):
        for slot in range(2):
            rcopy(pbuf.at[0, i], rbuf.at[slot, i], ss.at[slot * 4 + i], sr.at[slot * 4 + i], sib).wait_send()
        qcopy(away, i).wait_send()


def local(activations, norm_gain, key_weight, value_weight, key_cot, value_cot, blocks):
    any_spec = pl.BlockSpec(memory_space=pl.ANY)
    vmem_spec = pl.BlockSpec(memory_space=pltpu.VMEM)
    dma = pltpu.SemaphoreType.DMA
    key_out, value_out, grad, bg = pl.pallas_call(
        body,
        out_shape=(
            jax.ShapeDtypeStruct((TOK, 256), BF16),
            jax.ShapeDtypeStruct((TOK, 256), BF16),
            jax.ShapeDtypeStruct((TOK, 2048), BF16),
            jax.ShapeDtypeStruct((16, 64, 128), F32),
        ),
        in_specs=[any_spec] * 6 + [pl.BlockSpec(memory_space=pltpu.SMEM)],
        out_specs=(vmem_spec,) * 4,
        scratch_shapes=[
            pltpu.VMEM((4, 4, 4, 128, 512), BF16),
            pltpu.VMEM((TOK, D), BF16),
            pltpu.VMEM((D // 128, TOK, 128), BF16),
            pltpu.VMEM((1, D), F32),
            pltpu.VMEM((4, TOK, 128), BF16),
            pltpu.VMEM((TOK, 512), F32),
            pltpu.VMEM((4, 4, TOK, 512), BF16),
            pltpu.VMEM((2, 4, TOK, 512), BF16),
            pltpu.VMEM((4, TOK, 512), BF16),
            pltpu.VMEM((4, 4, 64, 128), F32),
            pltpu.VMEM((4, 4, 64, 128), BF16),
            pltpu.VMEM((4, 4, 64, 128), BF16),
            pltpu.VMEM((4, 64, 128), F32),
            pltpu.VMEM((4, 64, 128), BF16),
            pltpu.VMEM((4, 64, 128), BF16),
            pltpu.VMEM((4, 16, 128), F32),
            pltpu.VMEM((4, 16, 128), BF16),
            pltpu.VMEM((4, 16, 128), BF16),
            pltpu.VMEM((4, 4, 4, 16, 128), BF16),
            dma((7 + TOK // ROWS,)),
            dma((16, 4)),
            dma((16, 4)),
            dma((10,)),
            dma((10,)),
            dma((18,)),
            dma((18,)),
            dma((8,)),
            dma((8,)),
            dma((4,)),
            dma((4,)),
        ],
        compiler_params=pltpu.CompilerParams(
            collective_id=0, has_side_effects=True, vmem_limit_bytes=60 * 1024 * 1024
        ),
        name="kv_step",
    )(
        activations,
        norm_gain.reshape(1, D),
        key_weight.reshape(4, 128, 256),
        value_weight.reshape(4, 128, 256),
        key_cot,
        value_cot,
        blocks,
    )
    bg = bg.reshape(16, 64, 2, 64).transpose(2, 0, 1, 3).reshape(2, 16, 4096)
    return key_out, value_out, grad, bg


def solution(mesh):
    in_specs = (
        P(("fsdp", "replica"), None),
        P(),
        P("fsdp", "tensor"),
        P("fsdp", "tensor"),
        P(("fsdp", "replica"), "tensor"),
        P(("fsdp", "replica"), "tensor"),
        P(None, "tensor", None),
    )
    out_specs = (
        P(("fsdp", "replica"), "tensor"),
        P(("fsdp", "replica"), "tensor"),
        P(("fsdp", "replica"), "tensor"),
        P(None, "tensor", None),
    )
    return jax.shard_map(local, mesh=mesh, in_specs=in_specs, out_specs=out_specs, check_vma=False)
```

```python
import functools

import jax
import jax.numpy as jnp
from jax import lax
from jax.experimental import pallas as pl
from jax.experimental.pallas import tpu as pltpu
from jax.sharding import PartitionSpec as P

D = 8192
TOK = 384
EPS = 1e-05
F32 = jnp.float32
BF16 = jnp.bfloat16
ROWS = 64

AXP, AXM, AXFP, AXFM, BYP, BYM, BYFP, BYFM, AYP, AYM, AYFP, AYFM, BXP, BXM, BXFP, BXFM = range(16)
ZAP, ZAM, ZBP, ZBM, ZFP, ZFM = range(6)


def body(
    act_hbm, gain_hbm, kw_hbm, vw_hbm, kc_hbm, vc_hbm, blocks,
    key_out, value_out, grad_out, bg_out,
    wa, wb, act, normed, gain, cot, acc, pbuf, rbuf, qbuf,
    g32, s1, r1, p1, s2, r2, p2, s3, r3, tall,
    ld, xs, xr, zs, zr, bs, br, ss, sr, qs, qr,
):
    f = lax.axis_index("fsdp")
    t = lax.axis_index("tensor")
    y = lax.axis_index("replica")
    zh, x = f // 4, f % 4
    zl = t // 2

    def m4(v):
        return lax.rem(v + 4, 4)

    def xdev(d):
        return {"fsdp": zh * 4 + m4(x + d)}

    def ydev(d):
        return {"replica": m4(y + d)}

    def zdev(d):
        return {"fsdp": m4(zh + d) * 4 + x}

    sib = {"tensor": t + 1 - 2 * (t % 2)}
    zpair = {"tensor": lax.rem(t + 2, 4)}

    loads = []

    def load(src, dst):
        c = pltpu.make_async_copy(src, dst, ld.at[len(loads)])
        c.start()
        loads.append(c)

    for i, w_hbm in enumerate((kw_hbm, vw_hbm)):
        load(w_hbm.at[y, 0], wa.at[zh, y, x, :, pl.ds(i * 256, 256)])
        load(w_hbm.at[y, 1], wb.at[zh, x, y, :, pl.ds(i * 256, 256)])
    load(gain_hbm, gain)
    for i in range(4):
        load((kc_hbm, vc_hbm)[i // 2].at[:, pl.ds(i % 2 * 128, 128)], cot.at[i])
    first_rows = len(loads)
    for i in range(TOK // ROWS):
        load(act_hbm.at[pl.ds(i * ROWS, ROWS)], act.at[pl.ds(i * ROWS, ROWS)])

    barrier = pltpu.get_barrier_semaphore()
    peers = [xdev(1), xdev(-1), xdev(2), ydev(1), ydev(-1), ydev(2), zdev(1), zdev(-1), zdev(2), sib, zpair]
    for peer in peers:
        pl.semaphore_signal(barrier, inc=1, device_id=peer, device_id_type=pl.DeviceIdType.MESH)
    pl.semaphore_wait(barrier, len(peers))

    sent = []

    def rcopy(src, dst, a, b, dev):
        return pltpu.make_async_remote_copy(
            src_ref=src, dst_ref=dst, send_sem=a, recv_sem=b, device_id=dev,
            device_id_type=pl.DeviceIdType.MESH,
        )

    def piece(kind, zz, px, py):
        if kind in (AXP, AXM):
            return wa.at[zz, py, px]
        if kind == AXFP:
            return wa.at[zz, py, m4(px - 1), pl.ds(0, 32)]
        if kind == AXFM:
            return wa.at[zz, py, m4(px + 1), pl.ds(32, 32)]
        if kind in (BYP, BYM):
            return wb.at[zz, px, py]
        if kind == BYFP:
            return wb.at[zz, px, m4(py - 1), pl.ds(0, 32)]
        if kind == BYFM:
            return wb.at[zz, px, m4(py + 1), pl.ds(32, 32)]
        if kind in (AYP, AYM):
            return wa.at[zz, py]
        if kind == AYFP:
            return wa.at[zz, m4(py - 1), pl.ds(0, 2)]
        if kind == AYFM:
            return wa.at[zz, m4(py + 1), pl.ds(2, 2)]
        if kind in (BXP, BXM):
            return wb.at[zz, px]
        if kind == BXFP:
            return wb.at[zz, m4(px - 1), pl.ds(0, 2)]
        return wb.at[zz, m4(px + 1), pl.ds(2, 2)]

    along_x = (AXP, AXM, AXFP, AXFM, BXP, BXM, BXFP, BXFM)
    plus = (AXP, AXFP, BYP, BYFP, AYP, AYFP, BXP, BXFP)

    def xy(kind, zz, incoming):
        d = 1 if kind in plus else -1
        back = d if incoming else 0
        if kind in along_x:
            ref, dev = piece(kind, zz, m4(x - back), y), xdev(d)
        else:
            ref, dev = piece(kind, zz, x, m4(y - back)), ydev(d)
        return rcopy(ref, ref, xs.at[kind, zz], xr.at[kind, zz], dev)

    def send(zz, *kinds):
        for kind in kinds:
            c = xy(kind, zz, False)
            c.start()
            sent.append(c)

    def recv(zz, *kinds):
        for kind in kinds:
            xy(kind, zz, True).wait_recv()

    def along_z(kind, incoming):
        d = 1 if kind in (ZAP, ZBP, ZFP) else -1
        pz = m4(zh - d) if incoming else zh
        if kind in (ZAP, ZAM):
            ref = wa.at[pz, y, x]
        elif kind in (ZBP, ZBM):
            ref = wb.at[pz, x, y]
        elif kind == ZFP:
            ref = wa.at[m4(pz - 1), y, x]
        else:
            ref = wb.at[m4(pz + 1), x, y]
        return rcopy(ref, ref, zs.at[kind], zr.at[kind], zdev(d))

    def zsend(*kinds):
        for kind in kinds:
            c = along_z(kind, False)
            c.start()
            sent.append(c)

    def zrecv(*kinds):
        for kind in kinds:
            along_z(kind, True).wait_recv()

    def lanes(rows):
        return lax.broadcasted_iota(jnp.int32, (rows, 128), 1) < 64

    def norm_rows(i):
        loads[first_rows + i].wait()
        low = lanes(16)

        @pl.loop(0, ROWS // 16)
        def _(k):
            rows = pl.ds(pl.multiple_of(i * ROWS + k * 16, 16), 16)
            total = jnp.zeros((16, 128), F32)
            for j in range(D // 512):
                v = act[rows, pl.ds(j * 512, 512)].astype(F32)
                v = v * v
                total = total + ((v[:, 0:128] + v[:, 128:256]) + (v[:, 256:384] + v[:, 384:512]))
            inv = lax.rsqrt(jnp.sum(total, axis=1, keepdims=True) / D + EPS)

            def tile(zz, xx, q):
                cols = pl.ds((zz * 16 + xx * 4 + q) * 128, 128)
                return act[rows, cols].astype(F32) * inv * gain[:, cols]

            for zz in range(4):
                for hx in range(2):
                    for hq in range(2):
                        ee, eo = tile(zz, 2 * hx, 2 * hq), tile(zz, 2 * hx, 2 * hq + 1)
                        oe, oo = tile(zz, 2 * hx + 1, 2 * hq), tile(zz, 2 * hx + 1, 2 * hq + 1)
                        ree, roe, roo = pltpu.roll(ee, 64, 1), pltpu.roll(oe, 64, 1), pltpu.roll(oo, 64, 1)
                        a0, b0 = (zz * 4 + 2 * hq) * 2 + hx, ((4 + zz) * 4 + 2 * hx) * 2 + hq
                        normed[a0, rows] = jnp.where(low, ee, roe).astype(BF16)
                        normed[a0 + 2, rows] = jnp.where(low, eo, roo).astype(BF16)
                        normed[b0, rows] = jnp.where(low, ree, eo).astype(BF16)
                        normed[b0 + 2, rows] = jnp.where(low, roe, oo).astype(BF16)

    def block_entry(p, n):
        row, column = blocks[p, 0, n], blocks[p, 1, n]
        zz, xx, q, odd = lax.div(row, 32), lax.rem(lax.div(row, 8), 4), lax.rem(lax.div(row, 2), 4), lax.rem(row, 2)
        in_a = zz * 8 + q * 2 + lax.div(xx, 2)
        in_b = 32 + zz * 8 + xx * 2 + lax.div(q, 2)
        left = normed[in_a * (1 - odd) + in_b * odd]
        half = lax.rem(xx, 2) * (1 - odd) + lax.rem(q, 2) * odd
        right = cot[2 * p + lax.div(column, 2)]
        full = lax.dot_general(left, right, (((0,), (0,)), ((), ())), preferred_element_type=F32)
        low = half.astype(F32)
        half = full[64:] * low + full[:64] * (1.0 - low)
        column_odd = lax.rem(column, 2).astype(F32)
        move = column_odd if p == 0 else 1.0 - column_odd
        return pltpu.roll(half, 64, 1) * move + half * (1.0 - move)

    def block_products(lo, hi):
        low = lanes(64)

        @pl.loop(lo, hi)
        def _(n):
            value = jnp.where(low, block_entry(0, n), block_entry(1, n))
            g32[n // 4, n % 4] = value
            s1[n // 4, n % 4] = value.astype(BF16)

    away = lax.rem(t + 2, 4)

    def sib_index(zz, ab, i):
        return (zz // 2 - zl) * (zz // 2 - zl) * 8 + ab * 4 + i

    def sibcopy(zz, ab, i):
        n = sib_index(zz, ab, i)
        return rcopy(pbuf.at[zz, ab, i], rbuf.at[n], ss.at[n], sr.at[n], sib)

    def qcopy(ab, i):
        return rcopy(pbuf.at[away, ab, i], qbuf.at[ab * 4 + i], qs.at[ab * 4 + i], qr.at[ab * 4 + i], zpair)

    def rwait(slot, ab, i):
        n = slot * 8 + ab * 4 + i
        rcopy(rbuf.at[n], rbuf.at[n], ss.at[n], sr.at[n], sib).wait_recv()

    def unit(zz, ab, i):
        w = (wa, wb)[ab][zz, i].reshape(256, 512)
        tile = ((ab * 4 + zz) * 4 + i) * 2
        left = jnp.concatenate([normed[tile], normed[tile + 1]], axis=1)
        acc[...] += jnp.dot(left, w, preferred_element_type=F32)
        both = jnp.concatenate([cot[j] for j in range(4)], axis=1)
        part = lax.dot_general(both, w, (((1,), (1,)), ((), ())), preferred_element_type=F32)
        pbuf[zz, ab, i] = part.astype(BF16)

        @pl.when(lax.rem(zz + t, 2) == 1)
        def _():
            sibcopy(zz, ab, i).start()

    def combine(zz, ab, i):
        @pl.when(zz == away)
        def _():
            rwait(1, ab, i)
            pbuf[zz, ab, i] = (pbuf[zz, ab, i].astype(F32) + rbuf[8 + ab * 4 + i].astype(F32)).astype(BF16)
            qcopy(ab, i).start()

    waiting = []

    def units(zz, d):
        for ab, i in ((0, m4(y + d)), (1, m4(x + d))):
            unit(zz, ab, i)
            while waiting:
                combine(*waiting.pop())
            waiting.append((zz, ab, i))

    dist = (1, -1, 2)

    def bg_copy(stage, d, incoming):
        back = d if incoming else 0
        axis = (0, 1, 2, 2, 1, 0)[stage]
        me = (y, x, zh)[axis]
        dev = (ydev, xdev, zdev)[axis](d)
        sender = m4(me - back)
        target = m4(sender + d)
        if stage < 3:
            src, dst = (s1, s2, s3)[stage].at[target], (r1, r2, r3)[stage].at[sender]
        else:
            where = [y, x, zh]
            where[axis] = sender
            src = dst = tall.at[tuple(where[: axis + 1])]
        i = stage * 3 + dist.index(d)
        return rcopy(src, dst, bs.at[i], br.at[i], dev)

    def bg_send(stage):
        for d in dist:
            c = bg_copy(stage, d, False)
            c.start()
            sent.append(c)

    def bg_recv(stage):
        for d in dist:
            bg_copy(stage, d, True).wait_recv()

    def bg_sum(stage):
        bg_recv(stage)
        if stage == 0:
            total = g32[y]
            for d in dist:
                total = total + r1[m4(y - d)].astype(F32)
            p1[...] = total
            s2[...] = total.astype(BF16)
        elif stage == 1:
            total = p1[x]
            for d in dist:
                total = total + r2[m4(x - d)].astype(F32)
            total = total.reshape(4, 16, 128)
            p2[...] = total
            s3[...] = total.astype(BF16)
        else:
            total = p2[zh]
            for d in dist:
                total = total + r3[m4(zh - d)].astype(F32)
            tall[y, x, zh] = total.astype(BF16)
        bg_send(stage + 1)

    own_away = (zh // 2 - zl) * (zh // 2 - zl)
    step = 1 - 2 * (zh % 2)
    partner, near, far = m4(zh + step), m4(zh - step), m4(zh + 2)
    p0_, p1_ = zh, own_away * partner + (1 - own_away) * near
    p2_ = own_away * near + (1 - own_away) * far
    p3_ = own_away * far + (1 - own_away) * partner
    adjacent = own_away * near + (1 - own_away) * partner

    def small_forward(zz):
        recv(zz, AXP, BYP)
        send(zz, AXFP, BYFP)
        recv(zz, AXM, BYM)
        send(zz, AXFM, BYFM)

    def big(zz):
        recv(zz, AXFP, AXFM)
        send(zz, AYP, AYM)
        recv(zz, BYFP, BYFM)
        send(zz, BXP, BXM)

    def big_forward(zz):
        recv(zz, AYP, BXP)
        send(zz, AYFP, BXFP)
        recv(zz, AYM, BXM)
        send(zz, AYFM, BXFM)

    def big_end(zz):
        recv(zz, AYFP, AYFM, BXFP, BXFM)

    for i in range(4):
        loads[i].wait()
    zsend(ZAP, ZAM, ZBP, ZBM)
    send(p0_, AXP, AXM, BYP, BYM)
    acc[...] = jnp.zeros_like(acc)
    loads[4].wait()
    norm_rows(0)
    norm_rows(1)
    small_forward(p0_)
    norm_rows(2)
    norm_rows(3)
    zrecv(ZAP, ZAM)
    zsend(ZFP)
    send(p1_, AXP, AXM)
    send(adjacent, AXP, AXM)
    norm_rows(4)
    big(p0_)
    zrecv(ZBP, ZBM)
    zsend(ZFM)
    send(p1_, BYP, BYM)
    send(adjacent, BYP, BYM)
    norm_rows(5)
    for i in range(5, first_rows):
        loads[i].wait()
    units(p0_, 0)
    small_forward(p1_)
    zrecv(ZFP, ZFM)
    send(far, AXP, AXM, BYP, BYM)
    small_forward(adjacent)
    big(p1_)
    units(p1_, 0)
    small_forward(far)
    big_forward(p0_)
    big(p2_)
    units(p2_, 0)
    block_products(0, 8)
    big_forward(p1_)
    units(p1_, 1)
    units(p1_, -1)
    big(p3_)
    block_products(8, 16)
    bg_send(0)
    big_end(p0_)
    units(p0_, 1)
    units(p0_, -1)
    big_forward(p2_)
    units(p2_, 1)
    units(p2_, -1)
    big_end(p1_)
    units(p1_, 2)
    bg_sum(0)
    units(p0_, 2)
    units(p3_, 0)
    big_forward(p3_)
    bg_sum(1)
    big_end(p2_)
    units(p2_, 2)
    bg_sum(2)
    units(p3_, 1)
    units(p3_, -1)
    bg_recv(3)
    bg_send(4)
    big_end(p3_)
    units(p3_, 2)
    combine(*waiting.pop())
    bg_recv(4)
    bg_send(5)
    key_out[...] = acc[:, 0:256].astype(BF16)
    value_out[...] = acc[:, 256:512].astype(BF16)
    for ab in range(2):
        for i in range(4):
            rwait(0, ab, i)
            n = ab * 4 + i
            rcopy(qbuf.at[n], qbuf.at[n], qs.at[n], qr.at[n], zpair).wait_recv()

    @pl.loop(0, TOK // 16)
    def _(k):
        rows = pl.ds(pl.multiple_of(k * 16, 16), 16)
        low = lanes(16)

        def tile(ab, i, half):
            cols = pl.ds(half * 128, 128)
            n = ab * 4 + i
            return pbuf[t, ab, i, rows, cols].astype(F32) + rbuf[n, rows, cols].astype(F32) + qbuf[n, rows, cols].astype(F32)

        for hx in range(2):
            for hq in range(2):
                for b in range(2):
                    a_tile = tile(0, 2 * hq + b, hx)
                    a_tiles = (a_tile, pltpu.roll(a_tile, 64, 1))
                    for a in range(2):
                        b_tile = tile(1, 2 * hx + a, hq)
                        if b == 0:
                            b_tile = pltpu.roll(b_tile, 64, 1)
                        cols = pl.ds(((2 * hx + a) * 4 + 2 * hq + b) * 128, 128)
                        grad_out[rows, cols] = jnp.where(low, a_tiles[a], b_tile).astype(BF16)

    bg_recv(5)
    bg_out[...] = tall[...].astype(F32).reshape(16, 64, 128)

    for c in sent:
        c.wait_send()
    for n in range(16):
        rcopy(pbuf.at[0, 0, 0], rbuf.at[n], ss.at[n], sr.at[n], sib).wait_send()
    for ab in range(2):
        for i in range(4):
            qcopy(ab, i).wait_send()


def local(activations, norm_gain, key_weight, value_weight, key_cot, value_cot, blocks):
    any_spec = pl.BlockSpec(memory_space=pl.ANY)
    vmem_spec = pl.BlockSpec(memory_space=pltpu.VMEM)
    dma = pltpu.SemaphoreType.DMA
    key_out, value_out, grad, bg = pl.pallas_call(
        body,
        out_shape=(
            jax.ShapeDtypeStruct((TOK, 256), BF16),
            jax.ShapeDtypeStruct((TOK, 256), BF16),
            jax.ShapeDtypeStruct((TOK, 2048), BF16),
            jax.ShapeDtypeStruct((16, 64, 128), F32),
        ),
        in_specs=[any_spec] * 6 + [pl.BlockSpec(memory_space=pltpu.SMEM)],
        out_specs=(vmem_spec,) * 4,
        scratch_shapes=[
            pltpu.VMEM((4, 4, 4, 64, 512), BF16),
            pltpu.VMEM((4, 4, 4, 64, 512), BF16),
            pltpu.VMEM((TOK, D), BF16),
            pltpu.VMEM((D // 128, TOK, 128), BF16),
            pltpu.VMEM((1, D), F32),
            pltpu.VMEM((4, TOK, 128), BF16),
            pltpu.VMEM((TOK, 512), F32),
            pltpu.VMEM((4, 2, 4, TOK, 256), BF16),
            pltpu.VMEM((16, TOK, 256), BF16),
            pltpu.VMEM((8, TOK, 256), BF16),
            pltpu.VMEM((4, 4, 64, 128), F32),
            pltpu.VMEM((4, 4, 64, 128), BF16),
            pltpu.VMEM((4, 4, 64, 128), BF16),
            pltpu.VMEM((4, 64, 128), F32),
            pltpu.VMEM((4, 64, 128), BF16),
            pltpu.VMEM((4, 64, 128), BF16),
            pltpu.VMEM((4, 16, 128), F32),
            pltpu.VMEM((4, 16, 128), BF16),
            pltpu.VMEM((4, 16, 128), BF16),
            pltpu.VMEM((4, 4, 4, 16, 128), BF16),
            dma((9 + TOK // ROWS,)),
            dma((16, 4)),
            dma((16, 4)),
            dma((6,)),
            dma((6,)),
            dma((18,)),
            dma((18,)),
            dma((16,)),
            dma((16,)),
            dma((8,)),
            dma((8,)),
        ],
        compiler_params=pltpu.CompilerParams(
            collective_id=0, has_side_effects=True, vmem_limit_bytes=60 * 1024 * 1024
        ),
        name="kv_step",
    )(
        activations,
        norm_gain.reshape(1, D),
        key_weight.reshape(4, 2, 64, 256),
        value_weight.reshape(4, 2, 64, 256),
        key_cot,
        value_cot,
        blocks.transpose(0, 2, 1),
    )
    bg = bg.reshape(16, 64, 2, 64).transpose(2, 0, 1, 3).reshape(2, 16, 4096)
    return key_out, value_out, grad, bg


def solution(mesh):
    in_specs = (
        P(("fsdp", "replica"), None),
        P(),
        P("fsdp", "tensor"),
        P("fsdp", "tensor"),
        P(("fsdp", "replica"), "tensor"),
        P(("fsdp", "replica"), "tensor"),
        P(None, "tensor", None),
    )
    out_specs = (
        P(("fsdp", "replica"), "tensor"),
        P(("fsdp", "replica"), "tensor"),
        P(("fsdp", "replica"), "tensor"),
        P(None, "tensor", None),
    )
    return jax.shard_map(local, mesh=mesh, in_specs=in_specs, out_specs=out_specs, check_vma=False)
```

```python
import functools

import jax
import jax.numpy as jnp
from jax import lax
from jax.experimental import pallas as pl
from jax.experimental.pallas import tpu as pltpu
from jax.sharding import PartitionSpec as P

D = 8192
TOK = 384
EPS = 1e-05
F32 = jnp.float32
BF16 = jnp.bfloat16
ROWS = 64

AXP, AXM, AXFP, AXFM, BYP, BYM, BYFP, BYFM = range(8)
AYP0, AYP1, AYM0, AYM1, AYFP, AYFM, BXP0, BXP1, BXM0, BXM1, BXFP, BXFM = range(8, 20)
ZAP, ZAM, ZBP, ZBM, ZFP, ZFM = range(6)


def body(
    act_hbm, gain_hbm, kw_hbm, vw_hbm, kc_hbm, vc_hbm, blocks,
    key_out, value_out, grad_out, bg_out,
    wa, wb, act, normed, gain, cot, acc, pbuf, rbuf, qbuf,
    g32, s1, r1, p1, s2, r2, p2, s3, r3, tall, gall,
    ld, xs, xr, zs, zr, bs, br, ss, sr, qs, qr,
):
    f = lax.axis_index("fsdp")
    t = lax.axis_index("tensor")
    y = lax.axis_index("replica")
    zh, x = f // 4, f % 4
    zl = t // 2

    def m4(v):
        return lax.rem(v + 4, 4)

    def xdev(d):
        return {"fsdp": zh * 4 + m4(x + d)}

    def ydev(d):
        return {"replica": m4(y + d)}

    def zdev(d):
        return {"fsdp": m4(zh + d) * 4 + x}

    sib = {"tensor": t + 1 - 2 * (t % 2)}
    zpair = {"tensor": lax.rem(t + 2, 4)}

    loads = []

    def load(src, dst):
        c = pltpu.make_async_copy(src, dst, ld.at[len(loads)])
        c.start()
        loads.append(c)

    for i, w_hbm in enumerate((kw_hbm, vw_hbm)):
        load(w_hbm.at[y, 0], wa.at[zh, y, x, :, pl.ds(i * 256, 256)])
        load(w_hbm.at[y, 1], wb.at[zh, x, y, :, pl.ds(i * 256, 256)])
    load(gain_hbm, gain)
    for i in range(4):
        load((kc_hbm, vc_hbm)[i // 2].at[:, pl.ds(i % 2 * 128, 128)], cot.at[i])
    first_rows = len(loads)
    for i in range(TOK // ROWS):
        load(act_hbm.at[pl.ds(i * ROWS, ROWS)], act.at[pl.ds(i * ROWS, ROWS)])

    barrier = pltpu.get_barrier_semaphore()
    peers = [xdev(1), xdev(-1), xdev(2), ydev(1), ydev(-1), ydev(2), zdev(1), zdev(-1), zdev(2), sib, zpair]
    for peer in peers:
        pl.semaphore_signal(barrier, inc=1, device_id=peer, device_id_type=pl.DeviceIdType.MESH)
    pl.semaphore_wait(barrier, len(peers))

    sent = []

    def rcopy(src, dst, a, b, dev):
        return pltpu.make_async_remote_copy(
            src_ref=src, dst_ref=dst, send_sem=a, recv_sem=b, device_id=dev,
            device_id_type=pl.DeviceIdType.MESH,
        )

    def piece(kind, zz, px, py):
        if kind in (AXP, AXM):
            return wa.at[zz, py, px]
        if kind == AXFP:
            return wa.at[zz, py, m4(px - 1), pl.ds(0, 32)]
        if kind == AXFM:
            return wa.at[zz, py, m4(px + 1), pl.ds(32, 32)]
        if kind in (BYP, BYM):
            return wb.at[zz, px, py]
        if kind == BYFP:
            return wb.at[zz, px, m4(py - 1), pl.ds(0, 32)]
        if kind == BYFM:
            return wb.at[zz, px, m4(py + 1), pl.ds(32, 32)]
        if kind in (AYP0, AYM0):
            return wa.at[zz, py, pl.ds(0, 2)]
        if kind in (AYP1, AYM1):
            return wa.at[zz, py, pl.ds(2, 2)]
        if kind == AYFP:
            return wa.at[zz, m4(py - 1), pl.ds(0, 2)]
        if kind == AYFM:
            return wa.at[zz, m4(py + 1), pl.ds(2, 2)]
        if kind in (BXP0, BXM0):
            return wb.at[zz, px, pl.ds(0, 2)]
        if kind in (BXP1, BXM1):
            return wb.at[zz, px, pl.ds(2, 2)]
        if kind == BXFP:
            return wb.at[zz, m4(px - 1), pl.ds(0, 2)]
        return wb.at[zz, m4(px + 1), pl.ds(2, 2)]

    along_x = (AXP, AXM, AXFP, AXFM, BXP0, BXP1, BXM0, BXM1, BXFP, BXFM)
    plus = (AXP, AXFP, BYP, BYFP, AYP0, AYP1, AYFP, BXP0, BXP1, BXFP)

    def xy(kind, zz, incoming):
        d = 1 if kind in plus else -1
        back = d if incoming else 0
        if kind in along_x:
            ref, dev = piece(kind, zz, m4(x - back), y), xdev(d)
        else:
            ref, dev = piece(kind, zz, x, m4(y - back)), ydev(d)
        return rcopy(ref, ref, xs.at[kind, zz], xr.at[kind, zz], dev)

    def send(zz, *kinds):
        for kind in kinds:
            c = xy(kind, zz, False)
            c.start()
            sent.append(c)

    def recv(zz, *kinds):
        for kind in kinds:
            xy(kind, zz, True).wait_recv()

    def along_z(kind, incoming):
        d = 1 if kind in (ZAP, ZBP, ZFP) else -1
        pz = m4(zh - d) if incoming else zh
        if kind in (ZAP, ZAM):
            ref = wa.at[pz, y, x]
        elif kind in (ZBP, ZBM):
            ref = wb.at[pz, x, y]
        elif kind == ZFP:
            ref = wa.at[m4(pz - 1), y, x]
        else:
            ref = wb.at[m4(pz + 1), x, y]
        return rcopy(ref, ref, zs.at[kind], zr.at[kind], zdev(d))

    def zsend(*kinds):
        for kind in kinds:
            c = along_z(kind, False)
            c.start()
            sent.append(c)

    def zrecv(*kinds):
        for kind in kinds:
            along_z(kind, True).wait_recv()

    def lanes(rows):
        return lax.broadcasted_iota(jnp.int32, (rows, 128), 1) < 64

    def norm_rows(i):
        loads[first_rows + i].wait()
        low = lanes(16)

        @pl.loop(0, ROWS // 16)
        def _(k):
            rows = pl.ds(pl.multiple_of(i * ROWS + k * 16, 16), 16)
            total = jnp.zeros((16, 128), F32)
            for j in range(D // 512):
                v = act[rows, pl.ds(j * 512, 512)].astype(F32)
                v = v * v
                total = total + ((v[:, 0:128] + v[:, 128:256]) + (v[:, 256:384] + v[:, 384:512]))
            inv = lax.rsqrt(jnp.sum(total, axis=1, keepdims=True) / D + EPS)

            def tile(zz, xx, q):
                cols = pl.ds((zz * 16 + xx * 4 + q) * 128, 128)
                return act[rows, cols].astype(F32) * inv * gain[:, cols]

            for zz in range(4):
                for hx in range(2):
                    for hq in range(2):
                        ee, eo = tile(zz, 2 * hx, 2 * hq), tile(zz, 2 * hx, 2 * hq + 1)
                        oe, oo = tile(zz, 2 * hx + 1, 2 * hq), tile(zz, 2 * hx + 1, 2 * hq + 1)
                        ree, roe, roo = pltpu.roll(ee, 64, 1), pltpu.roll(oe, 64, 1), pltpu.roll(oo, 64, 1)
                        a0, b0 = (zz * 4 + 2 * hq) * 2 + hx, ((4 + zz) * 4 + 2 * hx) * 2 + hq
                        normed[a0, rows] = jnp.where(low, ee, roe).astype(BF16)
                        normed[a0 + 2, rows] = jnp.where(low, eo, roo).astype(BF16)
                        normed[b0, rows] = jnp.where(low, ree, eo).astype(BF16)
                        normed[b0 + 2, rows] = jnp.where(low, roe, oo).astype(BF16)

    def block_entry(p, n):
        row, column = blocks[p, 0, n], blocks[p, 1, n]
        zz, xx, q, odd = lax.div(row, 32), lax.rem(lax.div(row, 8), 4), lax.rem(lax.div(row, 2), 4), lax.rem(row, 2)
        in_a = zz * 8 + q * 2 + lax.div(xx, 2)
        in_b = 32 + zz * 8 + xx * 2 + lax.div(q, 2)
        left = normed[in_a * (1 - odd) + in_b * odd]
        half = lax.rem(xx, 2) * (1 - odd) + lax.rem(q, 2) * odd
        right = cot[2 * p + lax.div(column, 2)]
        full = lax.dot_general(left, right, (((0,), (0,)), ((), ())), preferred_element_type=F32)
        low = half.astype(F32)
        half = full[64:] * low + full[:64] * (1.0 - low)
        column_odd = lax.rem(column, 2).astype(F32)
        move = column_odd if p == 0 else 1.0 - column_odd
        return pltpu.roll(half, 64, 1) * move + half * (1.0 - move)

    def block_products(lo, hi):
        low = lanes(64)

        @pl.loop(lo, hi)
        def _(n):
            value = jnp.where(low, block_entry(0, n), block_entry(1, n))
            g32[n // 4, n % 4] = value
            s1[n // 4, n % 4] = value.astype(BF16)

    away = lax.rem(t + 2, 4)

    def sib_index(zz, ab, i):
        return (zz // 2 - zl) * (zz // 2 - zl) * 8 + ab * 4 + i

    def sibcopy(zz, ab, i):
        n = sib_index(zz, ab, i)
        return rcopy(pbuf.at[zz, ab, i], rbuf.at[n], ss.at[n], sr.at[n], sib)

    def qcopy(ab, i):
        return rcopy(pbuf.at[away, ab, i], qbuf.at[ab * 4 + i], qs.at[ab * 4 + i], qr.at[ab * 4 + i], zpair)

    def rwait(slot, ab, i):
        n = slot * 8 + ab * 4 + i
        rcopy(rbuf.at[n], rbuf.at[n], ss.at[n], sr.at[n], sib).wait_recv()

    def unit(zz, ab, i):
        w = (wa, wb)[ab][zz, i].reshape(256, 512)
        tile = ((ab * 4 + zz) * 4 + i) * 2
        left = jnp.concatenate([normed[tile], normed[tile + 1]], axis=1)
        acc[...] += jnp.dot(left, w, preferred_element_type=F32)
        both = jnp.concatenate([cot[j] for j in range(4)], axis=1)
        part = lax.dot_general(both, w, (((1,), (1,)), ((), ())), preferred_element_type=F32)
        pbuf[zz, ab, i] = part.astype(BF16)

        @pl.when(lax.rem(zz + t, 2) == 1)
        def _():
            sibcopy(zz, ab, i).start()

    def combine(zz, ab, i):
        @pl.when(zz == away)
        def _():
            rwait(1, ab, i)
            pbuf[zz, ab, i] = (pbuf[zz, ab, i].astype(F32) + rbuf[8 + ab * 4 + i].astype(F32)).astype(BF16)
            qcopy(ab, i).start()

    waiting = []

    def units(zz, d):
        for ab, i in ((0, m4(y + d)), (1, m4(x + d))):
            unit(zz, ab, i)
            while waiting:
                combine(*waiting.pop())
            waiting.append((zz, ab, i))

    dist = (1, -1, 2)

    def bg_copy(stage, d, incoming):
        back = d if incoming else 0
        axis = (0, 1, 2, 2, 1, 0)[stage]
        me = (y, x, zh)[axis]
        dev = (ydev, xdev, zdev)[axis](d)
        sender = m4(me - back)
        target = m4(sender + d)
        if stage < 3:
            src, dst = (s1, s2, s3)[stage].at[target], (r1, r2, r3)[stage].at[sender]
        else:
            where = [y, x, zh]
            where[axis] = sender
            src = dst = tall.at[tuple(where[: axis + 1])]
        i = stage * 3 + dist.index(d)
        return rcopy(src, dst, bs.at[i], br.at[i], dev)

    def bg_send(stage):
        for d in dist:
            c = bg_copy(stage, d, False)
            c.start()
            sent.append(c)

    def bg_recv(stage):
        for d in dist:
            bg_copy(stage, d, True).wait_recv()

    def bg_sum(stage):
        bg_recv(stage)
        if stage == 0:
            total = g32[y]
            for d in dist:
                total = total + r1[m4(y - d)].astype(F32)
            p1[...] = total
            s2[...] = total.astype(BF16)
        elif stage == 1:
            total = p1[x]
            for d in dist:
                total = total + r2[m4(x - d)].astype(F32)
            total = total.reshape(4, 16, 128)
            p2[...] = total
            s3[...] = total.astype(BF16)
        else:
            total = p2[zh]
            for d in dist:
                total = total + r3[m4(zh - d)].astype(F32)
            tall[y, x, zh] = total.astype(BF16)
        bg_send(stage + 1)

    own_away = (zh // 2 - zl) * (zh // 2 - zl)
    step = 1 - 2 * (zh % 2)
    partner, near, far = m4(zh + step), m4(zh - step), m4(zh + 2)
    p0_, p1_ = zh, own_away * partner + (1 - own_away) * near
    p2_ = own_away * near + (1 - own_away) * far
    p3_ = own_away * far + (1 - own_away) * partner
    adjacent = own_away * near + (1 - own_away) * partner

    def small_a(zz):
        recv(zz, AXP)
        send(zz, AXFP)
        recv(zz, AXM)
        send(zz, AXFM)

    def small_b(zz):
        recv(zz, BYP)
        send(zz, BYFP)
        recv(zz, BYM)
        send(zz, BYFM)

    def big_first(zz):
        recv(zz, AXFP, AXFM)
        send(zz, AYP0, AYM1)
        recv(zz, BYFP, BYFM)
        send(zz, BXP0, BXM1)

    def big_second(zz):
        send(zz, AYP1, AYM0, BXP1, BXM0)

    def big_forward(zz):
        for got, kind in ((AYP0, AYFP), (BXP0, BXFP), (AYM1, AYFM), (BXM1, BXFM)):
            recv(zz, got)
            send(zz, kind)

    def big_middle(zz):
        recv(zz, AYP1, AYM0, BXP1, BXM0)

    def big_end(zz):
        recv(zz, AYFP, AYFM, BXFP, BXFM)

    for i in range(4):
        loads[i].wait()
    zsend(ZAP, ZAM, ZBP, ZBM)
    send(p0_, AXP, AXM, BYP, BYM)
    loads[4].wait()
    norm_rows(0)
    norm_rows(1)
    small_a(p0_)
    small_b(p0_)
    norm_rows(2)
    zrecv(ZAP, ZAM)
    zsend(ZFP)
    send(p1_, AXP, AXM)
    send(adjacent, AXP, AXM)
    norm_rows(3)
    big_first(p0_)
    zrecv(ZBP, ZBM)
    zsend(ZFM)
    send(p1_, BYP, BYM)
    send(adjacent, BYP, BYM)
    big_second(p0_)
    norm_rows(4)
    norm_rows(5)
    small_a(p1_)
    small_a(adjacent)
    for i in range(5, first_rows):
        loads[i].wait()
    block_products(0, 4)
    zrecv(ZFP, ZFM)
    send(far, AXP, AXM, BYP, BYM)
    big_forward(p0_)
    block_products(4, 6)
    small_b(p1_)
    small_b(adjacent)
    block_products(6, 8)
    big_first(p1_)
    block_products(8, 12)
    small_a(far)
    small_b(far)
    big_second(p1_)
    block_products(12, 16)
    bg_send(0)
    acc[...] = jnp.zeros_like(acc)
    units(p1_, 0)
    units(p0_, 0)
    big_middle(p0_)
    big_first(p2_)
    units(p2_, 0)
    units(p0_, 1)
    units(p0_, -1)
    big_forward(p1_)
    big_middle(p1_)
    big_second(p2_)
    units(p1_, 1)
    units(p1_, -1)
    bg_sum(0)
    big_end(p0_)
    units(p0_, 2)
    big_first(p3_)
    big_end(p1_)
    units(p1_, 2)
    bg_sum(1)
    big_forward(p2_)
    big_second(p3_)
    big_middle(p2_)
    units(p2_, 1)
    units(p2_, -1)
    big_forward(p3_)
    big_end(p2_)
    units(p2_, 2)
    bg_sum(2)
    units(p3_, 0)
    big_middle(p3_)
    units(p3_, 1)
    units(p3_, -1)
    bg_recv(3)
    bg_send(4)
    big_end(p3_)
    units(p3_, 2)
    combine(*waiting.pop())
    bg_recv(4)
    bg_send(5)
    key_out[...] = acc[:, 0:256].astype(BF16)
    value_out[...] = acc[:, 256:512].astype(BF16)
    for ab in range(2):
        for i in range(4):
            rwait(0, ab, i)
            n = ab * 4 + i
            rcopy(qbuf.at[n], qbuf.at[n], qs.at[n], qr.at[n], zpair).wait_recv()

    @pl.loop(0, TOK // 16)
    def _(k):
        rows = pl.ds(pl.multiple_of(k * 16, 16), 16)
        low = lanes(16)

        def tile(ab, i, half):
            cols = pl.ds(half * 128, 128)
            n = ab * 4 + i
            return pbuf[t, ab, i, rows, cols].astype(F32) + rbuf[n, rows, cols].astype(F32) + qbuf[n, rows, cols].astype(F32)

        for hx in range(2):
            for hq in range(2):
                for b in range(2):
                    a_tile = tile(0, 2 * hq + b, hx)
                    a_tiles = (a_tile, pltpu.roll(a_tile, 64, 1))
                    for a in range(2):
                        b_tile = tile(1, 2 * hx + a, hq)
                        if b == 0:
                            b_tile = pltpu.roll(b_tile, 64, 1)
                        cols = pl.ds(((2 * hx + a) * 4 + 2 * hq + b) * 128, 128)
                        grad_out[rows, cols] = jnp.where(low, a_tiles[a], b_tile).astype(BF16)

    bg_recv(5)
    gall[...] = tall[...].astype(F32).reshape(1024, 128)
    low8 = lanes(8)
    for h in range(2):
        for k in range(32):
            even = gall[pl.ds(h * 512 + 2 * k, 8, stride=64), :]
            odd = gall[pl.ds(h * 512 + 2 * k + 1, 8, stride=64), :]
            rows, cols = pl.ds(h * 8, 8), pl.ds(k * 128, 128)
            bg_out[0, rows, cols] = jnp.where(low8, even, pltpu.roll(odd, 64, 1))
            bg_out[1, rows, cols] = jnp.where(low8, pltpu.roll(even, 64, 1), odd)

    for c in sent:
        c.wait_send()
    for n in range(16):
        rcopy(pbuf.at[0, 0, 0], rbuf.at[n], ss.at[n], sr.at[n], sib).wait_send()
    for ab in range(2):
        for i in range(4):
            qcopy(ab, i).wait_send()


def local(activations, norm_gain, key_weight, value_weight, key_cot, value_cot, blocks):
    any_spec = pl.BlockSpec(memory_space=pl.ANY)
    vmem_spec = pl.BlockSpec(memory_space=pltpu.VMEM)
    dma = pltpu.SemaphoreType.DMA
    key_out, value_out, grad, bg = pl.pallas_call(
        body,
        out_shape=(
            pltpu.VMEM((TOK, 256), BF16),
            pltpu.VMEM((TOK, 256), BF16),
            pltpu.VMEM((TOK, 2048), BF16),
            pltpu.VMEM((2, 16, 4096), F32),
        ),
        in_specs=[any_spec] * 6 + [pl.BlockSpec(memory_space=pltpu.SMEM)],
        out_specs=(vmem_spec,) * 4,
        scratch_shapes=[
            pltpu.VMEM((4, 4, 4, 64, 512), BF16),
            pltpu.VMEM((4, 4, 4, 64, 512), BF16),
            pltpu.VMEM((TOK, D), BF16),
            pltpu.VMEM((D // 128, TOK, 128), BF16),
            pltpu.VMEM((1, D), F32),
            pltpu.VMEM((4, TOK, 128), BF16),
            pltpu.VMEM((TOK, 512), F32),
            pltpu.VMEM((4, 2, 4, TOK, 256), BF16),
            pltpu.VMEM((16, TOK, 256), BF16),
            pltpu.VMEM((8, TOK, 256), BF16),
            pltpu.VMEM((4, 4, 64, 128), F32),
            pltpu.VMEM((4, 4, 64, 128), BF16),
            pltpu.VMEM((4, 4, 64, 128), BF16),
            pltpu.VMEM((4, 64, 128), F32),
            pltpu.VMEM((4, 64, 128), BF16),
            pltpu.VMEM((4, 64, 128), BF16),
            pltpu.VMEM((4, 16, 128), F32),
            pltpu.VMEM((4, 16, 128), BF16),
            pltpu.VMEM((4, 16, 128), BF16),
            pltpu.VMEM((4, 4, 4, 16, 128), BF16),
            pltpu.VMEM((1024, 128), F32),
            dma((9 + TOK // ROWS,)),
            dma((20, 4)),
            dma((20, 4)),
            dma((6,)),
            dma((6,)),
            dma((18,)),
            dma((18,)),
            dma((16,)),
            dma((16,)),
            dma((8,)),
            dma((8,)),
        ],
        compiler_params=pltpu.CompilerParams(
            collective_id=0, has_side_effects=True, vmem_limit_bytes=60 * 1024 * 1024
        ),
        name="kv_step",
    )(
        activations,
        norm_gain.reshape(1, D),
        key_weight.reshape(4, 2, 64, 256),
        value_weight.reshape(4, 2, 64, 256),
        key_cot,
        value_cot,
        blocks.transpose(0, 2, 1),
    )
    return key_out, value_out, grad, bg


def solution(mesh):
    in_specs = (
        P(("fsdp", "replica"), None),
        P(),
        P("fsdp", "tensor"),
        P("fsdp", "tensor"),
        P(("fsdp", "replica"), "tensor"),
        P(("fsdp", "replica"), "tensor"),
        P(None, "tensor", None),
    )
    out_specs = (
        P(("fsdp", "replica"), "tensor"),
        P(("fsdp", "replica"), "tensor"),
        P(("fsdp", "replica"), "tensor"),
        P(None, "tensor", None),
    )
    return jax.shard_map(local, mesh=mesh, in_specs=in_specs, out_specs=out_specs, check_vma=False)
```

```python
import functools

import jax
import jax.numpy as jnp
from jax import lax
from jax.experimental import pallas as pl
from jax.experimental.pallas import tpu as pltpu
from jax.sharding import PartitionSpec as P

D = 8192
TOK = 384
EPS = 1e-05
F32 = jnp.float32
BF16 = jnp.bfloat16
ROWS = 64

AXP, AXM, AXFP, AXFM, BYP, BYM, BYFP, BYFM = range(8)
AYP0, AYP1, AYM0, AYM1, AYFP, AYFM, BXP0, BXP1, BXM0, BXM1, BXFP, BXFM = range(8, 20)
ZAP, ZAM, ZBP, ZBM, ZFP, ZFM = range(6)


def body(
    act_hbm, gain_hbm, kw_hbm, vw_hbm, kc_hbm, vc_hbm, blocks,
    key_out, value_out, grad_out, bg_out,
    wa, wb, act, normed, gain, cot, acc, pbuf, rbuf, qbuf,
    g32, s1, r1, p1, s2, r2, gz, tall, gall,
    ld, xs, xr, zs, zr, bs, br, ss, sr, qs, qr,
):
    f = lax.axis_index("fsdp")
    t = lax.axis_index("tensor")
    y = lax.axis_index("replica")
    zh, x = f // 4, f % 4
    zl = t // 2

    def m4(v):
        return lax.rem(v + 4, 4)

    def xdev(d):
        return {"fsdp": zh * 4 + m4(x + d)}

    def ydev(d):
        return {"replica": m4(y + d)}

    def zdev(d):
        return {"fsdp": m4(zh + d) * 4 + x}

    sib = {"tensor": t + 1 - 2 * (t % 2)}
    zpair = {"tensor": lax.rem(t + 2, 4)}

    loads = []

    def load(src, dst):
        c = pltpu.make_async_copy(src, dst, ld.at[len(loads)])
        c.start()
        loads.append(c)

    for i, w_hbm in enumerate((kw_hbm, vw_hbm)):
        load(w_hbm.at[y, 0], wa.at[zh, y, x, :, pl.ds(i * 256, 256)])
        load(w_hbm.at[y, 1], wb.at[zh, x, y, :, pl.ds(i * 256, 256)])
    load(gain_hbm, gain)
    for i in range(4):
        load((kc_hbm, vc_hbm)[i // 2].at[:, pl.ds(i % 2 * 128, 128)], cot.at[i])
    first_rows = len(loads)
    for i in range(TOK // ROWS):
        load(act_hbm.at[pl.ds(i * ROWS, ROWS)], act.at[pl.ds(i * ROWS, ROWS)])

    barrier = pltpu.get_barrier_semaphore()
    peers = [xdev(1), xdev(-1), xdev(2), ydev(1), ydev(-1), ydev(2), zdev(1), zdev(-1), sib, zpair]
    for peer in peers:
        pl.semaphore_signal(barrier, inc=1, device_id=peer, device_id_type=pl.DeviceIdType.MESH)
    pl.semaphore_wait(barrier, len(peers))

    sent = []

    def rcopy(src, dst, a, b, dev):
        return pltpu.make_async_remote_copy(
            src_ref=src, dst_ref=dst, send_sem=a, recv_sem=b, device_id=dev,
            device_id_type=pl.DeviceIdType.MESH,
        )

    def piece(kind, zz, px, py):
        if kind in (AXP, AXM):
            return wa.at[zz, py, px]
        if kind == AXFP:
            return wa.at[zz, py, m4(px - 1), pl.ds(0, 32)]
        if kind == AXFM:
            return wa.at[zz, py, m4(px + 1), pl.ds(32, 32)]
        if kind in (BYP, BYM):
            return wb.at[zz, px, py]
        if kind == BYFP:
            return wb.at[zz, px, m4(py - 1), pl.ds(0, 32)]
        if kind == BYFM:
            return wb.at[zz, px, m4(py + 1), pl.ds(32, 32)]
        if kind in (AYP0, AYM0):
            return wa.at[zz, py, pl.ds(0, 2)]
        if kind in (AYP1, AYM1):
            return wa.at[zz, py, pl.ds(2, 2)]
        if kind == AYFP:
            return wa.at[zz, m4(py - 1), pl.ds(0, 2)]
        if kind == AYFM:
            return wa.at[zz, m4(py + 1), pl.ds(2, 2)]
        if kind in (BXP0, BXM0):
            return wb.at[zz, px, pl.ds(0, 2)]
        if kind in (BXP1, BXM1):
            return wb.at[zz, px, pl.ds(2, 2)]
        if kind == BXFP:
            return wb.at[zz, m4(px - 1), pl.ds(0, 2)]
        return wb.at[zz, m4(px + 1), pl.ds(2, 2)]

    along_x = (AXP, AXM, AXFP, AXFM, BXP0, BXP1, BXM0, BXM1, BXFP, BXFM)
    plus = (AXP, AXFP, BYP, BYFP, AYP0, AYP1, AYFP, BXP0, BXP1, BXFP)

    def xy(kind, zz, incoming):
        d = 1 if kind in plus else -1
        back = d if incoming else 0
        if kind in along_x:
            ref, dev = piece(kind, zz, m4(x - back), y), xdev(d)
        else:
            ref, dev = piece(kind, zz, x, m4(y - back)), ydev(d)
        return rcopy(ref, ref, xs.at[kind, zz], xr.at[kind, zz], dev)

    def send(zz, *kinds):
        for kind in kinds:
            c = xy(kind, zz, False)
            c.start()
            sent.append(c)

    def recv(zz, *kinds):
        for kind in kinds:
            xy(kind, zz, True).wait_recv()

    def along_z(kind, incoming):
        d = 1 if kind in (ZAP, ZBP, ZFP) else -1
        pz = m4(zh - d) if incoming else zh
        if kind in (ZAP, ZAM):
            ref = wa.at[pz, y, x]
        elif kind in (ZBP, ZBM):
            ref = wb.at[pz, x, y]
        elif kind == ZFP:
            ref = wa.at[m4(pz - 1), y, x]
        else:
            ref = wb.at[m4(pz + 1), x, y]
        return rcopy(ref, ref, zs.at[kind], zr.at[kind], zdev(d))

    def zsend(*kinds):
        for kind in kinds:
            c = along_z(kind, False)
            c.start()
            sent.append(c)

    def zrecv(*kinds):
        for kind in kinds:
            along_z(kind, True).wait_recv()

    def lanes(rows):
        return lax.broadcasted_iota(jnp.int32, (rows, 128), 1) < 64

    def norm_rows(i):
        loads[first_rows + i].wait()
        low = lanes(16)

        @pl.loop(0, ROWS // 16)
        def _(k):
            rows = pl.ds(pl.multiple_of(i * ROWS + k * 16, 16), 16)
            total = jnp.zeros((16, 128), F32)
            for j in range(D // 512):
                v = act[rows, pl.ds(j * 512, 512)].astype(F32)
                v = v * v
                total = total + ((v[:, 0:128] + v[:, 128:256]) + (v[:, 256:384] + v[:, 384:512]))
            inv = lax.rsqrt(jnp.sum(total, axis=1, keepdims=True) / D + EPS)

            def tile(zz, xx, q):
                cols = pl.ds((zz * 16 + xx * 4 + q) * 128, 128)
                return act[rows, cols].astype(F32) * inv * gain[:, cols]

            for zz in range(4):
                for hx in range(2):
                    for hq in range(2):
                        ee, eo = tile(zz, 2 * hx, 2 * hq), tile(zz, 2 * hx, 2 * hq + 1)
                        oe, oo = tile(zz, 2 * hx + 1, 2 * hq), tile(zz, 2 * hx + 1, 2 * hq + 1)
                        ree, roe, roo = pltpu.roll(ee, 64, 1), pltpu.roll(oe, 64, 1), pltpu.roll(oo, 64, 1)
                        a0, b0 = (zz * 4 + 2 * hq) * 2 + hx, ((4 + zz) * 4 + 2 * hx) * 2 + hq
                        normed[a0, rows] = jnp.where(low, ee, roe).astype(BF16)
                        normed[a0 + 2, rows] = jnp.where(low, eo, roo).astype(BF16)
                        normed[b0, rows] = jnp.where(low, ree, eo).astype(BF16)
                        normed[b0 + 2, rows] = jnp.where(low, roe, oo).astype(BF16)

    def block_entry(p, n):
        row, column = blocks[p, 0, n], blocks[p, 1, n]
        zz, xx, q, odd = lax.div(row, 32), lax.rem(lax.div(row, 8), 4), lax.rem(lax.div(row, 2), 4), lax.rem(row, 2)
        in_a = zz * 8 + q * 2 + lax.div(xx, 2)
        in_b = 32 + zz * 8 + xx * 2 + lax.div(q, 2)
        left = normed[in_a * (1 - odd) + in_b * odd]
        half = lax.rem(xx, 2) * (1 - odd) + lax.rem(q, 2) * odd
        right = cot[2 * p + lax.div(column, 2)]
        full = lax.dot_general(left, right, (((0,), (0,)), ((), ())), preferred_element_type=F32)
        low = half.astype(F32)
        half = full[64:] * low + full[:64] * (1.0 - low)
        column_odd = lax.rem(column, 2).astype(F32)
        move = column_odd if p == 0 else 1.0 - column_odd
        return pltpu.roll(half, 64, 1) * move + half * (1.0 - move)

    def block_products(lo, hi):
        low = lanes(64)

        @pl.loop(lo, hi)
        def _(n):
            value = jnp.where(low, block_entry(0, n), block_entry(1, n))
            g32[n // 4, n % 4] = value
            s1[n // 4, n % 4] = value.astype(BF16)

    away = lax.rem(t + 2, 4)

    def sib_index(zz, ab, i):
        return (zz // 2 - zl) * (zz // 2 - zl) * 8 + ab * 4 + i

    def sibcopy(zz, ab, i):
        n = sib_index(zz, ab, i)
        return rcopy(pbuf.at[zz, ab, i], rbuf.at[n], ss.at[n], sr.at[n], sib)

    def qcopy(ab, i):
        return rcopy(pbuf.at[away, ab, i], qbuf.at[ab * 4 + i], qs.at[ab * 4 + i], qr.at[ab * 4 + i], zpair)

    def rwait(slot, ab, i):
        n = slot * 8 + ab * 4 + i
        rcopy(rbuf.at[n], rbuf.at[n], ss.at[n], sr.at[n], sib).wait_recv()

    def unit(zz, ab, i):
        w = (wa, wb)[ab][zz, i].reshape(256, 512)
        tile = ((ab * 4 + zz) * 4 + i) * 2
        left = jnp.concatenate([normed[tile], normed[tile + 1]], axis=1)
        acc[...] += jnp.dot(left, w, preferred_element_type=F32)
        both = jnp.concatenate([cot[j] for j in range(4)], axis=1)
        part = lax.dot_general(both, w, (((1,), (1,)), ((), ())), preferred_element_type=F32)
        pbuf[zz, ab, i] = part.astype(BF16)

        @pl.when(lax.rem(zz + t, 2) == 1)
        def _():
            sibcopy(zz, ab, i).start()

    def combine(zz, ab, i):
        @pl.when(zz == away)
        def _():
            rwait(1, ab, i)
            pbuf[zz, ab, i] = (pbuf[zz, ab, i].astype(F32) + rbuf[8 + ab * 4 + i].astype(F32)).astype(BF16)
            qcopy(ab, i).start()

    waiting = []

    def units(zz, d):
        for ab, i in ((0, m4(y + d)), (1, m4(x + d))):
            unit(zz, ab, i)
            while waiting:
                combine(*waiting.pop())
            waiting.append((zz, ab, i))

    dist = (1, -1, 2)

    def bg_copy(stage, d, incoming):
        back = d if incoming else 0
        over_x = stage in (1, 2)
        sender = m4((x if over_x else y) - back)
        target = m4(sender + d)
        dev = xdev(d) if over_x else ydev(d)
        if stage == 0:
            src, dst = s1.at[target], r1.at[sender]
        elif stage == 1:
            src, dst = s2.at[target], r2.at[sender]
        else:
            src = dst = tall.at[y, sender] if over_x else tall.at[sender]
        i = stage * 3 + dist.index(d)
        return rcopy(src, dst, bs.at[i], br.at[i], dev)

    def bg_send(stage):
        for d in dist:
            c = bg_copy(stage, d, False)
            c.start()
            sent.append(c)

    def bg_recv(stage):
        for d in dist:
            bg_copy(stage, d, True).wait_recv()

    turn = 2 * zl - 1

    def ring(k, incoming):
        ref = gz.at[m4(zh - (k + incoming) * turn)]
        return rcopy(ref, ref, bs.at[12 + k], br.at[12 + k], {"fsdp": m4(zh + turn) * 4 + x})

    def ring_send(k):
        c = ring(k, 0)
        c.start()
        sent.append(c)

    def ring_step(k):
        ring(k, 1).wait_recv()
        if k < 2:
            ring_send(k + 1)
            return
        total = gz[0].astype(F32)
        for i in range(1, 4):
            total = total + gz[i].astype(F32)
        tall[y, x] = total.astype(BF16)
        bg_send(2)

    def bg_sum(stage):
        bg_recv(stage)
        if stage == 0:
            total = g32[y]
            for d in dist:
                total = total + r1[m4(y - d)].astype(F32)
            p1[...] = total
            s2[...] = total.astype(BF16)
            bg_send(1)
        else:
            total = p1[x]
            for d in dist:
                total = total + r2[m4(x - d)].astype(F32)
            gz[zh] = total.astype(BF16)
            ring_send(0)

    own_away = (zh // 2 - zl) * (zh // 2 - zl)
    step = 1 - 2 * (zh % 2)
    partner, near, far = m4(zh + step), m4(zh - step), m4(zh + 2)
    p0_, p1_ = zh, own_away * partner + (1 - own_away) * near
    p2_ = own_away * near + (1 - own_away) * far
    p3_ = own_away * far + (1 - own_away) * partner
    adjacent = own_away * near + (1 - own_away) * partner

    def small_a(zz):
        recv(zz, AXP)
        send(zz, AXFP)
        recv(zz, AXM)
        send(zz, AXFM)

    def small_b(zz):
        recv(zz, BYP)
        send(zz, BYFP)
        recv(zz, BYM)
        send(zz, BYFM)

    def big_first(zz):
        recv(zz, AXFP, AXFM)
        send(zz, AYP0, AYM1)
        recv(zz, BYFP, BYFM)
        send(zz, BXP0, BXM1)

    def big_second(zz):
        send(zz, AYP1, AYM0, BXP1, BXM0)

    def big_forward(zz):
        for got, kind in ((AYP0, AYFP), (BXP0, BXFP), (AYM1, AYFM), (BXM1, BXFM)):
            recv(zz, got)
            send(zz, kind)

    def big_middle(zz):
        recv(zz, AYP1, AYM0, BXP1, BXM0)

    def big_end(zz):
        recv(zz, AYFP, AYFM, BXFP, BXFM)

    for i in range(4):
        loads[i].wait()
    zsend(ZAP, ZAM, ZBP, ZBM)
    send(p0_, AXP, AXM, BYP, BYM)
    loads[4].wait()
    norm_rows(0)
    norm_rows(1)
    small_a(p0_)
    small_b(p0_)
    norm_rows(2)
    zrecv(ZAP, ZAM)
    zsend(ZFP)
    send(p1_, AXP, AXM)
    send(adjacent, AXP, AXM)
    norm_rows(3)
    big_first(p0_)
    zrecv(ZBP, ZBM)
    zsend(ZFM)
    send(p1_, BYP, BYM)
    send(adjacent, BYP, BYM)
    norm_rows(4)
    norm_rows(5)
    for i in range(5, first_rows):
        loads[i].wait()
    block_products(0, 5)
    small_a(p1_)
    small_b(p1_)
    block_products(5, 8)
    small_a(adjacent)
    small_b(adjacent)
    zrecv(ZFP, ZFM)
    send(far, AXP, AXM, BYP, BYM)
    acc[...] = jnp.zeros_like(acc)
    big_first(p1_)
    units(p1_, 0)
    units(p0_, 0)
    block_products(8, 11)
    small_a(far)
    small_b(far)
    big_second(p1_)
    block_products(11, 16)
    bg_send(0)
    big_first(p2_)
    units(p2_, 0)
    big_forward(p1_)
    big_second(p2_)
    bg_sum(0)
    big_middle(p1_)
    units(p1_, 1)
    units(p1_, -1)
    big_forward(p0_)
    big_end(p1_)
    units(p1_, 2)
    bg_sum(1)
    big_forward(p2_)
    big_second(p0_)
    big_middle(p2_)
    units(p2_, 1)
    units(p2_, -1)
    ring_step(0)
    big_first(p3_)
    big_end(p2_)
    units(p2_, 2)
    ring_step(1)
    big_second(p3_)
    big_middle(p0_)
    big_end(p0_)
    units(p0_, 1)
    units(p0_, -1)
    units(p0_, 2)
    ring_step(2)
    big_forward(p3_)
    units(p3_, 0)
    bg_recv(2)
    bg_send(3)
    big_middle(p3_)
    units(p3_, 1)
    units(p3_, -1)
    big_end(p3_)
    units(p3_, 2)
    combine(*waiting.pop())
    key_out[...] = acc[:, 0:256].astype(BF16)
    value_out[...] = acc[:, 256:512].astype(BF16)
    for ab in range(2):
        for i in range(4):
            rwait(0, ab, i)
            n = ab * 4 + i
            rcopy(qbuf.at[n], qbuf.at[n], qs.at[n], qr.at[n], zpair).wait_recv()

    @pl.loop(0, TOK // 16)
    def _(k):
        rows = pl.ds(pl.multiple_of(k * 16, 16), 16)
        low = lanes(16)

        def tile(ab, i, half):
            cols = pl.ds(half * 128, 128)
            n = ab * 4 + i
            return pbuf[t, ab, i, rows, cols].astype(F32) + rbuf[n, rows, cols].astype(F32) + qbuf[n, rows, cols].astype(F32)

        for hx in range(2):
            for hq in range(2):
                for b in range(2):
                    a_tile = tile(0, 2 * hq + b, hx)
                    a_tiles = (a_tile, pltpu.roll(a_tile, 64, 1))
                    for a in range(2):
                        b_tile = tile(1, 2 * hx + a, hq)
                        if b == 0:
                            b_tile = pltpu.roll(b_tile, 64, 1)
                        cols = pl.ds(((2 * hx + a) * 4 + 2 * hq + b) * 128, 128)
                        grad_out[rows, cols] = jnp.where(low, a_tiles[a], b_tile).astype(BF16)

    bg_recv(3)
    gall[...] = tall[...].astype(F32).reshape(1024, 128)
    low8 = lanes(8)
    for h in range(2):
        for k in range(32):
            even = gall[pl.ds(h * 512 + 2 * k, 8, stride=64), :]
            odd = gall[pl.ds(h * 512 + 2 * k + 1, 8, stride=64), :]
            rows, cols = pl.ds(h * 8, 8), pl.ds(k * 128, 128)
            bg_out[0, rows, cols] = jnp.where(low8, even, pltpu.roll(odd, 64, 1))
            bg_out[1, rows, cols] = jnp.where(low8, pltpu.roll(even, 64, 1), odd)

    for c in sent:
        c.wait_send()
    for n in range(16):
        rcopy(pbuf.at[0, 0, 0], rbuf.at[n], ss.at[n], sr.at[n], sib).wait_send()
    for ab in range(2):
        for i in range(4):
            qcopy(ab, i).wait_send()


def local(activations, norm_gain, key_weight, value_weight, key_cot, value_cot, blocks):
    any_spec = pl.BlockSpec(memory_space=pl.ANY)
    vmem_spec = pl.BlockSpec(memory_space=pltpu.VMEM)
    dma = pltpu.SemaphoreType.DMA
    key_out, value_out, grad, bg = pl.pallas_call(
        body,
        out_shape=(
            pltpu.VMEM((TOK, 256), BF16),
            pltpu.VMEM((TOK, 256), BF16),
            pltpu.VMEM((TOK, 2048), BF16),
            pltpu.VMEM((2, 16, 4096), F32),
        ),
        in_specs=[any_spec] * 6 + [pl.BlockSpec(memory_space=pltpu.SMEM)],
        out_specs=(vmem_spec,) * 4,
        scratch_shapes=[
            pltpu.VMEM((4, 4, 4, 64, 512), BF16),
            pltpu.VMEM((4, 4, 4, 64, 512), BF16),
            pltpu.VMEM((TOK, D), BF16),
            pltpu.VMEM((D // 128, TOK, 128), BF16),
            pltpu.VMEM((1, D), F32),
            pltpu.VMEM((4, TOK, 128), BF16),
            pltpu.VMEM((TOK, 512), F32),
            pltpu.VMEM((4, 2, 4, TOK, 256), BF16),
            pltpu.VMEM((16, TOK, 256), BF16),
            pltpu.VMEM((8, TOK, 256), BF16),
            pltpu.VMEM((4, 4, 64, 128), F32),
            pltpu.VMEM((4, 4, 64, 128), BF16),
            pltpu.VMEM((4, 4, 64, 128), BF16),
            pltpu.VMEM((4, 64, 128), F32),
            pltpu.VMEM((4, 64, 128), BF16),
            pltpu.VMEM((4, 64, 128), BF16),
            pltpu.VMEM((4, 64, 128), BF16),
            pltpu.VMEM((4, 4, 64, 128), BF16),
            pltpu.VMEM((1024, 128), F32),
            dma((9 + TOK // ROWS,)),
            dma((20, 4)),
            dma((20, 4)),
            dma((6,)),
            dma((6,)),
            dma((15,)),
            dma((15,)),
            dma((16,)),
            dma((16,)),
            dma((8,)),
            dma((8,)),
        ],
        compiler_params=pltpu.CompilerParams(
            collective_id=0, has_side_effects=True, vmem_limit_bytes=60 * 1024 * 1024
        ),
        name="kv_step",
    )(
        activations,
        norm_gain.reshape(1, D),
        key_weight.reshape(4, 2, 64, 256),
        value_weight.reshape(4, 2, 64, 256),
        key_cot,
        value_cot,
        blocks.transpose(0, 2, 1),
    )
    return key_out, value_out, grad, bg


def solution(mesh):
    in_specs = (
        P(("fsdp", "replica"), None),
        P(),
        P("fsdp", "tensor"),
        P("fsdp", "tensor"),
        P(("fsdp", "replica"), "tensor"),
        P(("fsdp", "replica"), "tensor"),
        P(None, "tensor", None),
    )
    out_specs = (
        P(("fsdp", "replica"), "tensor"),
        P(("fsdp", "replica"), "tensor"),
        P(("fsdp", "replica"), "tensor"),
        P(None, "tensor", None),
    )
    return jax.shard_map(local, mesh=mesh, in_specs=in_specs, out_specs=out_specs, check_vma=False)
```

```python
import functools

import jax
import jax.numpy as jnp
from jax import lax
from jax.experimental import pallas as pl
from jax.experimental.pallas import tpu as pltpu
from jax.sharding import PartitionSpec as P

D = 8192
TOK = 384
EPS = 1e-05
F32 = jnp.float32
BF16 = jnp.bfloat16
ROWS = 64

AXP, AXM, AXFP, AXFM, BYP, BYM, BYFP, BYFM = range(8)
AYP0, AYP1, AYM0, AYM1, AYFP, AYFM, BXP0, BXP1, BXM0, BXM1, BXFP, BXFM = range(8, 20)
ZAP, ZAM, ZBP, ZBM, ZFP, ZFM = range(6)


def body(
    act_hbm, gain_hbm, kw_hbm, vw_hbm, kc_hbm, vc_hbm, blocks,
    key_out, value_out, grad_out, bg_out,
    wa, wb, act, normed, gain, cot, acc, pbuf, rbuf, qbuf,
    g32, s1, r1, p1, s2, r2, gz, tall, gall,
    ld, xs, xr, zs, zr, bs, br, ss, sr, qs, qr,
):
    f = lax.axis_index("fsdp")
    t = lax.axis_index("tensor")
    y = lax.axis_index("replica")
    zh, x = f // 4, f % 4
    zl = t // 2

    def m4(v):
        return lax.rem(v + 4, 4)

    def xdev(d):
        return {"fsdp": zh * 4 + m4(x + d)}

    def ydev(d):
        return {"replica": m4(y + d)}

    def zdev(d):
        return {"fsdp": m4(zh + d) * 4 + x}

    sib = {"tensor": t + 1 - 2 * (t % 2)}
    zpair = {"tensor": lax.rem(t + 2, 4)}

    loads = []

    def load(src, dst):
        c = pltpu.make_async_copy(src, dst, ld.at[len(loads)])
        c.start()
        loads.append(c)

    for i, w_hbm in enumerate((kw_hbm, vw_hbm)):
        load(w_hbm.at[y, 0], wa.at[zh, y, x, :, pl.ds(i * 256, 256)])
        load(w_hbm.at[y, 1], wb.at[zh, x, y, :, pl.ds(i * 256, 256)])
    load(gain_hbm, gain)
    for i in range(4):
        load((kc_hbm, vc_hbm)[i // 2].at[:, pl.ds(i % 2 * 128, 128)], cot.at[i])
    first_rows = len(loads)
    for i in range(TOK // ROWS):
        load(act_hbm.at[pl.ds(i * ROWS, ROWS)], act.at[pl.ds(i * ROWS, ROWS)])

    barrier = pltpu.get_barrier_semaphore()
    peers = [xdev(1), xdev(-1), xdev(2), ydev(1), ydev(-1), ydev(2), zdev(1), zdev(-1), sib, zpair]
    for peer in peers:
        pl.semaphore_signal(barrier, inc=1, device_id=peer, device_id_type=pl.DeviceIdType.MESH)
    pl.semaphore_wait(barrier, len(peers))

    sent = []

    def rcopy(src, dst, a, b, dev):
        return pltpu.make_async_remote_copy(
            src_ref=src, dst_ref=dst, send_sem=a, recv_sem=b, device_id=dev,
            device_id_type=pl.DeviceIdType.MESH,
        )

    def piece(kind, zz, px, py):
        if kind in (AXP, AXM):
            return wa.at[zz, py, px]
        if kind == AXFP:
            return wa.at[zz, py, m4(px - 1), pl.ds(0, 32)]
        if kind == AXFM:
            return wa.at[zz, py, m4(px + 1), pl.ds(32, 32)]
        if kind in (BYP, BYM):
            return wb.at[zz, px, py]
        if kind == BYFP:
            return wb.at[zz, px, m4(py - 1), pl.ds(0, 32)]
        if kind == BYFM:
            return wb.at[zz, px, m4(py + 1), pl.ds(32, 32)]
        if kind in (AYP0, AYM0):
            return wa.at[zz, py, pl.ds(0, 2)]
        if kind in (AYP1, AYM1):
            return wa.at[zz, py, pl.ds(2, 2)]
        if kind == AYFP:
            return wa.at[zz, m4(py - 1), pl.ds(0, 2)]
        if kind == AYFM:
            return wa.at[zz, m4(py + 1), pl.ds(2, 2)]
        if kind in (BXP0, BXM0):
            return wb.at[zz, px, pl.ds(0, 2)]
        if kind in (BXP1, BXM1):
            return wb.at[zz, px, pl.ds(2, 2)]
        if kind == BXFP:
            return wb.at[zz, m4(px - 1), pl.ds(0, 2)]
        return wb.at[zz, m4(px + 1), pl.ds(2, 2)]

    along_x = (AXP, AXM, AXFP, AXFM, BXP0, BXP1, BXM0, BXM1, BXFP, BXFM)
    plus = (AXP, AXFP, BYP, BYFP, AYP0, AYP1, AYFP, BXP0, BXP1, BXFP)

    def xy(kind, zz, incoming):
        d = 1 if kind in plus else -1
        back = d if incoming else 0
        if kind in along_x:
            ref, dev = piece(kind, zz, m4(x - back), y), xdev(d)
        else:
            ref, dev = piece(kind, zz, x, m4(y - back)), ydev(d)
        return rcopy(ref, ref, xs.at[kind, zz], xr.at[kind, zz], dev)

    def send(zz, *kinds):
        for kind in kinds:
            c = xy(kind, zz, False)
            c.start()
            sent.append(c)

    def recv(zz, *kinds):
        for kind in kinds:
            xy(kind, zz, True).wait_recv()

    def along_z(kind, incoming):
        d = 1 if kind in (ZAP, ZBP, ZFP) else -1
        pz = m4(zh - d) if incoming else zh
        if kind in (ZAP, ZAM):
            ref = wa.at[pz, y, x]
        elif kind in (ZBP, ZBM):
            ref = wb.at[pz, x, y]
        elif kind == ZFP:
            ref = wa.at[m4(pz - 1), y, x]
        else:
            ref = wb.at[m4(pz + 1), x, y]
        return rcopy(ref, ref, zs.at[kind], zr.at[kind], zdev(d))

    def zsend(*kinds):
        for kind in kinds:
            c = along_z(kind, False)
            c.start()
            sent.append(c)

    def zrecv(*kinds):
        for kind in kinds:
            along_z(kind, True).wait_recv()

    def lanes(rows):
        return lax.broadcasted_iota(jnp.int32, (rows, 128), 1) < 64

    def norm_rows(i):
        loads[first_rows + i].wait()
        low = lanes(16)

        @pl.loop(0, ROWS // 16)
        def _(k):
            rows = pl.ds(pl.multiple_of(i * ROWS + k * 16, 16), 16)
            total = jnp.zeros((16, 128), F32)
            for j in range(D // 512):
                v = act[rows, pl.ds(j * 512, 512)].astype(F32)
                v = v * v
                total = total + ((v[:, 0:128] + v[:, 128:256]) + (v[:, 256:384] + v[:, 384:512]))
            inv = lax.rsqrt(jnp.sum(total, axis=1, keepdims=True) / D + EPS)

            def tile(zz, xx, q):
                cols = pl.ds((zz * 16 + xx * 4 + q) * 128, 128)
                return act[rows, cols].astype(F32) * inv * gain[:, cols]

            for zz in range(4):
                for hx in range(2):
                    for hq in range(2):
                        ee, eo = tile(zz, 2 * hx, 2 * hq), tile(zz, 2 * hx, 2 * hq + 1)
                        oe, oo = tile(zz, 2 * hx + 1, 2 * hq), tile(zz, 2 * hx + 1, 2 * hq + 1)
                        ree, roe, roo = pltpu.roll(ee, 64, 1), pltpu.roll(oe, 64, 1), pltpu.roll(oo, 64, 1)
                        a0, b0 = (zz * 4 + 2 * hq) * 2 + hx, ((4 + zz) * 4 + 2 * hx) * 2 + hq
                        normed[a0, rows] = jnp.where(low, ee, roe).astype(BF16)
                        normed[a0 + 2, rows] = jnp.where(low, eo, roo).astype(BF16)
                        normed[b0, rows] = jnp.where(low, ree, eo).astype(BF16)
                        normed[b0 + 2, rows] = jnp.where(low, roe, oo).astype(BF16)

    def block_entry(p, n):
        row, column = blocks[p, 0, n], blocks[p, 1, n]
        zz, xx, q, odd = lax.div(row, 32), lax.rem(lax.div(row, 8), 4), lax.rem(lax.div(row, 2), 4), lax.rem(row, 2)
        in_a = zz * 8 + q * 2 + lax.div(xx, 2)
        in_b = 32 + zz * 8 + xx * 2 + lax.div(q, 2)
        left = normed[in_a * (1 - odd) + in_b * odd]
        half = lax.rem(xx, 2) * (1 - odd) + lax.rem(q, 2) * odd
        right = cot[2 * p + lax.div(column, 2)]
        full = lax.dot_general(left, right, (((0,), (0,)), ((), ())), preferred_element_type=F32)
        low = half.astype(F32)
        half = full[64:] * low + full[:64] * (1.0 - low)
        column_odd = lax.rem(column, 2).astype(F32)
        move = column_odd if p == 0 else 1.0 - column_odd
        return pltpu.roll(half, 64, 1) * move + half * (1.0 - move)

    def block_products(lo, hi):
        low = lanes(64)

        @pl.loop(lo, hi)
        def _(n):
            value = jnp.where(low, block_entry(0, n), block_entry(1, n))
            g32[n // 4, n % 4] = value
            s1[n // 4, n % 4] = value.astype(BF16)

    away = lax.rem(t + 2, 4)

    def sib_index(zz, ab, i):
        return (zz // 2 - zl) * (zz // 2 - zl) * 8 + ab * 4 + i

    def sibcopy(zz, ab, i):
        n = sib_index(zz, ab, i)
        return rcopy(pbuf.at[zz, ab, i], rbuf.at[n], ss.at[n], sr.at[n], sib)

    def qcopy(ab, i):
        return rcopy(pbuf.at[away, ab, i], qbuf.at[ab * 4 + i], qs.at[ab * 4 + i], qr.at[ab * 4 + i], zpair)

    def unit(zz, ab, i):
        w = (wa, wb)[ab][zz, i].reshape(256, 512)
        tile = ((ab * 4 + zz) * 4 + i) * 2
        left = jnp.concatenate([normed[tile], normed[tile + 1]], axis=1)
        acc[...] += jnp.dot(left, w, preferred_element_type=F32)
        both = jnp.concatenate([cot[j] for j in range(4)], axis=1)
        part = lax.dot_general(both, w, (((1,), (1,)), ((), ())), preferred_element_type=F32)
        pbuf[zz, ab, i] = part.astype(BF16)

        @pl.when(lax.rem(zz + t, 2) == 1)
        def _():
            sibcopy(zz, ab, i).start()

    def combine(zz, ab, i):
        @pl.when(lax.rem(zz + t, 2) == 0)
        def _():
            n = sib_index(zz, ab, i)
            rcopy(rbuf.at[n], rbuf.at[n], ss.at[n], sr.at[n], sib).wait_recv()
            pbuf[zz, ab, i] = (pbuf[zz, ab, i].astype(F32) + rbuf[n].astype(F32)).astype(BF16)

        @pl.when(zz == away)
        def _():
            qcopy(ab, i).start()

    waiting = []

    def units(zz, d):
        for ab, i in ((0, m4(y + d)), (1, m4(x + d))):
            unit(zz, ab, i)
            while waiting:
                combine(*waiting.pop())
            waiting.append((zz, ab, i))

    dist = (1, -1, 2)

    def bg_copy(stage, d, incoming):
        back = d if incoming else 0
        over_x = stage in (1, 2)
        sender = m4((x if over_x else y) - back)
        target = m4(sender + d)
        dev = xdev(d) if over_x else ydev(d)
        if stage == 0:
            src, dst = s1.at[target], r1.at[sender]
        elif stage == 1:
            src, dst = s2.at[target], r2.at[sender]
        else:
            src = dst = tall.at[y, sender] if over_x else tall.at[sender]
        i = stage * 3 + dist.index(d)
        return rcopy(src, dst, bs.at[i], br.at[i], dev)

    def bg_send(stage):
        for d in dist:
            c = bg_copy(stage, d, False)
            c.start()
            sent.append(c)

    def bg_recv(stage):
        for d in dist:
            bg_copy(stage, d, True).wait_recv()

    turn = 2 * zl - 1

    def ring(k, incoming):
        ref = gz.at[m4(zh - (k + incoming) * turn)]
        return rcopy(ref, ref, bs.at[12 + k], br.at[12 + k], {"fsdp": m4(zh + turn) * 4 + x})

    def ring_send(k):
        c = ring(k, 0)
        c.start()
        sent.append(c)

    def ring_step(k):
        ring(k, 1).wait_recv()
        if k < 2:
            ring_send(k + 1)
            return
        total = gz[0].astype(F32)
        for i in range(1, 4):
            total = total + gz[i].astype(F32)
        tall[y, x] = total.astype(BF16)
        bg_send(2)

    def bg_sum(stage):
        bg_recv(stage)
        if stage == 0:
            total = g32[y]
            for d in dist:
                total = total + r1[m4(y - d)].astype(F32)
            p1[...] = total
            s2[...] = total.astype(BF16)
            bg_send(1)
        else:
            total = p1[x]
            for d in dist:
                total = total + r2[m4(x - d)].astype(F32)
            gz[zh] = total.astype(BF16)
            ring_send(0)

    own_away = (zh // 2 - zl) * (zh // 2 - zl)
    step = 1 - 2 * (zh % 2)
    partner, near, far = m4(zh + step), m4(zh - step), m4(zh + 2)
    p0_, p1_ = zh, own_away * partner + (1 - own_away) * near
    p2_ = own_away * near + (1 - own_away) * far
    p3_ = own_away * far + (1 - own_away) * partner
    adjacent = own_away * near + (1 - own_away) * partner

    def small_a(zz):
        recv(zz, AXP)
        send(zz, AXFP)
        recv(zz, AXM)
        send(zz, AXFM)

    def small_b(zz):
        recv(zz, BYP)
        send(zz, BYFP)
        recv(zz, BYM)
        send(zz, BYFM)

    def big_first(zz):
        recv(zz, AXFP, AXFM)
        send(zz, AYP0, AYM1)
        recv(zz, BYFP, BYFM)
        send(zz, BXP0, BXM1)

    def big_second(zz):
        send(zz, AYP1, AYM0, BXP1, BXM0)

    def big_forward(zz):
        for got, kind in ((AYP0, AYFP), (BXP0, BXFP), (AYM1, AYFM), (BXM1, BXFM)):
            recv(zz, got)
            send(zz, kind)

    def big_middle(zz):
        recv(zz, AYP1, AYM0, BXP1, BXM0)

    def big_end(zz):
        recv(zz, AYFP, AYFM, BXFP, BXFM)

    for i in range(4):
        loads[i].wait()
    zsend(ZAP, ZAM, ZBP, ZBM)
    send(p0_, AXP, AXM, BYP, BYM)
    loads[4].wait()
    norm_rows(0)
    norm_rows(1)
    small_a(p0_)
    small_b(p0_)
    norm_rows(2)
    zrecv(ZAP, ZAM)
    zsend(ZFP)
    send(p1_, AXP, AXM)
    send(adjacent, AXP, AXM)
    norm_rows(3)
    big_first(p0_)
    zrecv(ZBP, ZBM)
    zsend(ZFM)
    send(p1_, BYP, BYM)
    send(adjacent, BYP, BYM)
    norm_rows(4)
    norm_rows(5)
    for i in range(5, first_rows):
        loads[i].wait()
    block_products(0, 5)
    small_a(p1_)
    small_b(p1_)
    block_products(5, 8)
    small_a(adjacent)
    small_b(adjacent)
    zrecv(ZFP, ZFM)
    send(far, AXP, AXM, BYP, BYM)
    acc[...] = jnp.zeros_like(acc)
    big_first(p1_)
    units(p1_, 0)
    units(p0_, 0)
    block_products(8, 11)
    small_a(far)
    small_b(far)
    big_second(p1_)
    block_products(11, 16)
    bg_send(0)
    big_first(p2_)
    units(p2_, 0)
    big_forward(p1_)
    big_second(p2_)
    bg_sum(0)
    big_middle(p1_)
    units(p1_, 1)
    units(p1_, -1)
    big_forward(p0_)
    big_end(p1_)
    units(p1_, 2)
    bg_sum(1)
    big_forward(p2_)
    big_second(p0_)
    big_middle(p2_)
    units(p2_, 1)
    units(p2_, -1)
    ring_step(0)
    big_first(p3_)
    big_end(p2_)
    units(p2_, 2)
    ring_step(1)
    big_second(p3_)
    big_middle(p0_)
    big_end(p0_)
    units(p0_, 1)
    units(p0_, -1)
    units(p0_, 2)
    ring_step(2)
    big_forward(p3_)
    units(p3_, 0)
    bg_recv(2)
    bg_send(3)
    big_middle(p3_)
    units(p3_, 1)
    units(p3_, -1)
    big_end(p3_)
    units(p3_, 2)
    combine(*waiting.pop())
    key_out[...] = acc[:, 0:256].astype(BF16)
    value_out[...] = acc[:, 256:512].astype(BF16)
    bg_recv(3)
    gall[...] = tall[...].astype(F32).reshape(1024, 128)
    low8 = lanes(8)
    for h in range(2):
        for k in range(32):
            even = gall[pl.ds(h * 512 + 2 * k, 8, stride=64), :]
            odd = gall[pl.ds(h * 512 + 2 * k + 1, 8, stride=64), :]
            rows, cols = pl.ds(h * 8, 8), pl.ds(k * 128, 128)
            bg_out[0, rows, cols] = jnp.where(low8, even, pltpu.roll(odd, 64, 1))
            bg_out[1, rows, cols] = jnp.where(low8, pltpu.roll(even, 64, 1), odd)

    for ab in range(2):
        for i in range(4):
            n = ab * 4 + i
            rcopy(qbuf.at[n], qbuf.at[n], qs.at[n], qr.at[n], zpair).wait_recv()

    @pl.loop(0, TOK // 16)
    def _(k):
        rows = pl.ds(pl.multiple_of(k * 16, 16), 16)
        low = lanes(16)

        def tile(ab, i, half):
            cols = pl.ds(half * 128, 128)
            n = ab * 4 + i
            return pbuf[t, ab, i, rows, cols].astype(F32) + qbuf[n, rows, cols].astype(F32)

        for hx in range(2):
            for hq in range(2):
                for b in range(2):
                    a_tile = tile(0, 2 * hq + b, hx)
                    a_tiles = (a_tile, pltpu.roll(a_tile, 64, 1))
                    for a in range(2):
                        b_tile = tile(1, 2 * hx + a, hq)
                        if b == 0:
                            b_tile = pltpu.roll(b_tile, 64, 1)
                        cols = pl.ds(((2 * hx + a) * 4 + 2 * hq + b) * 128, 128)
                        grad_out[rows, cols] = jnp.where(low, a_tiles[a], b_tile).astype(BF16)

    for c in sent:
        c.wait_send()
    for n in range(16):
        rcopy(pbuf.at[0, 0, 0], rbuf.at[n], ss.at[n], sr.at[n], sib).wait_send()
    for ab in range(2):
        for i in range(4):
            qcopy(ab, i).wait_send()


def write_out(*refs):
    copies = [pltpu.make_async_copy(refs[i], refs[4 + i], refs[8].at[i]) for i in range(4)]
    for c in copies:
        c.start()
    for c in copies:
        c.wait()


def local(activations, norm_gain, key_weight, value_weight, key_cot, value_cot, blocks):
    any_spec = pl.BlockSpec(memory_space=pl.ANY)
    vmem_spec = pl.BlockSpec(memory_space=pltpu.VMEM)
    dma = pltpu.SemaphoreType.DMA
    key_out, value_out, grad, bg = pl.pallas_call(
        body,
        out_shape=(
            pltpu.VMEM((TOK, 256), BF16),
            pltpu.VMEM((TOK, 256), BF16),
            pltpu.VMEM((TOK, 2048), BF16),
            pltpu.VMEM((2, 16, 4096), F32),
        ),
        in_specs=[any_spec] * 6 + [pl.BlockSpec(memory_space=pltpu.SMEM)],
        out_specs=(vmem_spec,) * 4,
        scratch_shapes=[
            pltpu.VMEM((4, 4, 4, 64, 512), BF16),
            pltpu.VMEM((4, 4, 4, 64, 512), BF16),
            pltpu.VMEM((TOK, D), BF16),
            pltpu.VMEM((D // 128, TOK, 128), BF16),
            pltpu.VMEM((1, D), F32),
            pltpu.VMEM((4, TOK, 128), BF16),
            pltpu.VMEM((TOK, 512), F32),
            pltpu.VMEM((4, 2, 4, TOK, 256), BF16),
            pltpu.VMEM((16, TOK, 256), BF16),
            pltpu.VMEM((8, TOK, 256), BF16),
            pltpu.VMEM((4, 4, 64, 128), F32),
            pltpu.VMEM((4, 4, 64, 128), BF16),
            pltpu.VMEM((4, 4, 64, 128), BF16),
            pltpu.VMEM((4, 64, 128), F32),
            pltpu.VMEM((4, 64, 128), BF16),
            pltpu.VMEM((4, 64, 128), BF16),
            pltpu.VMEM((4, 64, 128), BF16),
            pltpu.VMEM((4, 4, 64, 128), BF16),
            pltpu.VMEM((1024, 128), F32),
            dma((9 + TOK // ROWS,)),
            dma((20, 4)),
            dma((20, 4)),
            dma((6,)),
            dma((6,)),
            dma((15,)),
            dma((15,)),
            dma((16,)),
            dma((16,)),
            dma((8,)),
            dma((8,)),
        ],
        compiler_params=pltpu.CompilerParams(
            collective_id=0, has_side_effects=True, vmem_limit_bytes=60 * 1024 * 1024
        ),
        name="kv_step",
    )(
        activations,
        norm_gain.reshape(1, D),
        key_weight.reshape(4, 2, 64, 256),
        value_weight.reshape(4, 2, 64, 256),
        key_cot,
        value_cot,
        blocks.transpose(0, 2, 1),
    )
    results = (key_out, value_out, grad, bg)
    return pl.pallas_call(
        write_out,
        out_shape=tuple(jax.ShapeDtypeStruct(r.shape, r.dtype) for r in results),
        in_specs=[any_spec] * 4,
        out_specs=(any_spec,) * 4,
        scratch_shapes=[dma((4,))],
        compiler_params=pltpu.CompilerParams(vmem_limit_bytes=1024 * 1024),
        name="write_out",
    )(*results)


def solution(mesh):
    in_specs = (
        P(("fsdp", "replica"), None),
        P(),
        P("fsdp", "tensor"),
        P("fsdp", "tensor"),
        P(("fsdp", "replica"), "tensor"),
        P(("fsdp", "replica"), "tensor"),
        P(None, "tensor", None),
    )
    out_specs = (
        P(("fsdp", "replica"), "tensor"),
        P(("fsdp", "replica"), "tensor"),
        P(("fsdp", "replica"), "tensor"),
        P(None, "tensor", None),
    )
    return jax.shard_map(local, mesh=mesh, in_specs=in_specs, out_specs=out_specs, check_vma=False)
```

```python
import functools

import jax
import jax.numpy as jnp
from jax import lax
from jax.experimental import pallas as pl
from jax.experimental.pallas import tpu as pltpu
from jax.sharding import PartitionSpec as P

D = 8192
TOK = 384
EPS = 1e-05
F32 = jnp.float32
BF16 = jnp.bfloat16
ROWS = 64

AXP, AXM, AXFP, AXFM, BYP, BYM, BYFP, BYFM = range(8)
AYP0, AYP1, AYM0, AYM1, AYFP, AYFM, BXP0, BXP1, BXM0, BXM1, BXFP, BXFM = range(8, 20)
ZAP, ZAM, ZBP, ZBM, ZFP, ZFM = range(6)


def body(
    act_hbm, gain_hbm, kw_hbm, vw_hbm, kc_hbm, vc_hbm, blocks,
    key_out, value_out, grad_out, bg_out,
    wa, wb, act, normed, gain, cot, acc, pbuf, rbuf, qbuf,
    g32, s1, r1, p1, s2, r2, gz, tall, gall,
    ld, xs, xr, zs, zr, bs, br, ss, sr, qs, qr,
):
    f = lax.axis_index("fsdp")
    t = lax.axis_index("tensor")
    y = lax.axis_index("replica")
    zh, x = f // 4, f % 4
    zl = t // 2

    def m4(v):
        return lax.rem(v + 4, 4)

    def xdev(d):
        return {"fsdp": zh * 4 + m4(x + d)}

    def ydev(d):
        return {"replica": m4(y + d)}

    def zdev(d):
        return {"fsdp": m4(zh + d) * 4 + x}

    sib = {"tensor": t + 1 - 2 * (t % 2)}
    zpair = {"tensor": lax.rem(t + 2, 4)}

    loads = []

    def load(src, dst):
        c = pltpu.make_async_copy(src, dst, ld.at[len(loads)])
        c.start()
        loads.append(c)

    for i, w_hbm in enumerate((kw_hbm, vw_hbm)):
        load(w_hbm.at[y, 0], wa.at[zh, y, x, :, pl.ds(i * 256, 256)])
        load(w_hbm.at[y, 1], wb.at[zh, x, y, :, pl.ds(i * 256, 256)])
    load(gain_hbm, gain)
    for i in range(4):
        load((kc_hbm, vc_hbm)[i // 2].at[:, pl.ds(i % 2 * 128, 128)], cot.at[i])
    first_rows = len(loads)
    for i in range(TOK // ROWS):
        load(act_hbm.at[pl.ds(i * ROWS, ROWS)], act.at[pl.ds(i * ROWS, ROWS)])

    barrier = pltpu.get_barrier_semaphore()
    peers = [xdev(1), xdev(-1), xdev(2), ydev(1), ydev(-1), ydev(2), zdev(1), zdev(-1), sib, zpair]
    for peer in peers:
        pl.semaphore_signal(barrier, inc=1, device_id=peer, device_id_type=pl.DeviceIdType.MESH)
    pl.semaphore_wait(barrier, len(peers))

    sent = []

    def rcopy(src, dst, a, b, dev):
        return pltpu.make_async_remote_copy(
            src_ref=src, dst_ref=dst, send_sem=a, recv_sem=b, device_id=dev,
            device_id_type=pl.DeviceIdType.MESH,
        )

    def piece(kind, zz, px, py):
        if kind in (AXP, AXM):
            return wa.at[zz, py, px]
        if kind == AXFP:
            return wa.at[zz, py, m4(px - 1), pl.ds(0, 32)]
        if kind == AXFM:
            return wa.at[zz, py, m4(px + 1), pl.ds(32, 32)]
        if kind in (BYP, BYM):
            return wb.at[zz, px, py]
        if kind == BYFP:
            return wb.at[zz, px, m4(py - 1), pl.ds(0, 32)]
        if kind == BYFM:
            return wb.at[zz, px, m4(py + 1), pl.ds(32, 32)]
        if kind in (AYP0, AYM0):
            return wa.at[zz, py, pl.ds(0, 2)]
        if kind in (AYP1, AYM1):
            return wa.at[zz, py, pl.ds(2, 2)]
        if kind == AYFP:
            return wa.at[zz, m4(py - 1), pl.ds(0, 2)]
        if kind == AYFM:
            return wa.at[zz, m4(py + 1), pl.ds(2, 2)]
        if kind in (BXP0, BXM0):
            return wb.at[zz, px, pl.ds(0, 2)]
        if kind in (BXP1, BXM1):
            return wb.at[zz, px, pl.ds(2, 2)]
        if kind == BXFP:
            return wb.at[zz, m4(px - 1), pl.ds(0, 2)]
        return wb.at[zz, m4(px + 1), pl.ds(2, 2)]

    along_x = (AXP, AXM, AXFP, AXFM, BXP0, BXP1, BXM0, BXM1, BXFP, BXFM)
    plus = (AXP, AXFP, BYP, BYFP, AYP0, AYP1, AYFP, BXP0, BXP1, BXFP)

    def xy(kind, zz, incoming):
        d = 1 if kind in plus else -1
        back = d if incoming else 0
        if kind in along_x:
            ref, dev = piece(kind, zz, m4(x - back), y), xdev(d)
        else:
            ref, dev = piece(kind, zz, x, m4(y - back)), ydev(d)
        return rcopy(ref, ref, xs.at[kind, zz], xr.at[kind, zz], dev)

    def send(zz, *kinds):
        for kind in kinds:
            c = xy(kind, zz, False)
            c.start()
            sent.append(c)

    def recv(zz, *kinds):
        for kind in kinds:
            xy(kind, zz, True).wait_recv()

    def along_z(kind, incoming):
        d = 1 if kind in (ZAP, ZBP, ZFP) else -1
        pz = m4(zh - d) if incoming else zh
        if kind in (ZAP, ZAM):
            ref = wa.at[pz, y, x]
        elif kind in (ZBP, ZBM):
            ref = wb.at[pz, x, y]
        elif kind == ZFP:
            ref = wa.at[m4(pz - 1), y, x]
        else:
            ref = wb.at[m4(pz + 1), x, y]
        return rcopy(ref, ref, zs.at[kind], zr.at[kind], zdev(d))

    def zsend(*kinds):
        for kind in kinds:
            c = along_z(kind, False)
            c.start()
            sent.append(c)

    def zrecv(*kinds):
        for kind in kinds:
            along_z(kind, True).wait_recv()

    def lanes(rows):
        return lax.broadcasted_iota(jnp.int32, (rows, 128), 1) < 64

    def norm_rows(i):
        loads[first_rows + i].wait()
        low = lanes(16)

        @pl.loop(0, ROWS // 16)
        def _(k):
            rows = pl.ds(pl.multiple_of(i * ROWS + k * 16, 16), 16)
            total = jnp.zeros((16, 128), F32)
            for j in range(D // 512):
                v = act[rows, pl.ds(j * 512, 512)].astype(F32)
                v = v * v
                total = total + ((v[:, 0:128] + v[:, 128:256]) + (v[:, 256:384] + v[:, 384:512]))
            inv = lax.rsqrt(jnp.sum(total, axis=1, keepdims=True) / D + EPS)

            def tile(zz, xx, q):
                cols = pl.ds((zz * 16 + xx * 4 + q) * 128, 128)
                return act[rows, cols].astype(F32) * inv * gain[:, cols]

            for zz in range(4):
                for hx in range(2):
                    for hq in range(2):
                        ee, eo = tile(zz, 2 * hx, 2 * hq), tile(zz, 2 * hx, 2 * hq + 1)
                        oe, oo = tile(zz, 2 * hx + 1, 2 * hq), tile(zz, 2 * hx + 1, 2 * hq + 1)
                        ree, roe, roo = pltpu.roll(ee, 64, 1), pltpu.roll(oe, 64, 1), pltpu.roll(oo, 64, 1)
                        a0, b0 = (zz * 4 + 2 * hq) * 2 + hx, ((4 + zz) * 4 + 2 * hx) * 2 + hq
                        normed[a0, rows] = jnp.where(low, ee, roe).astype(BF16)
                        normed[a0 + 2, rows] = jnp.where(low, eo, roo).astype(BF16)
                        normed[b0, rows] = jnp.where(low, ree, eo).astype(BF16)
                        normed[b0 + 2, rows] = jnp.where(low, roe, oo).astype(BF16)

    def block_entry(p, n):
        row, column = blocks[p, 0, n], blocks[p, 1, n]
        zz, xx, q, odd = lax.div(row, 32), lax.rem(lax.div(row, 8), 4), lax.rem(lax.div(row, 2), 4), lax.rem(row, 2)
        in_a = zz * 8 + q * 2 + lax.div(xx, 2)
        in_b = 32 + zz * 8 + xx * 2 + lax.div(q, 2)
        left = normed[in_a * (1 - odd) + in_b * odd]
        half = lax.rem(xx, 2) * (1 - odd) + lax.rem(q, 2) * odd
        right = cot[2 * p + lax.div(column, 2)]
        full = lax.dot_general(left, right, (((0,), (0,)), ((), ())), preferred_element_type=F32)
        low = half.astype(F32)
        half = full[64:] * low + full[:64] * (1.0 - low)
        column_odd = lax.rem(column, 2).astype(F32)
        move = column_odd if p == 0 else 1.0 - column_odd
        return pltpu.roll(half, 64, 1) * move + half * (1.0 - move)

    def block_products(lo, hi):
        low = lanes(64)

        @pl.loop(lo, hi)
        def _(n):
            value = jnp.where(low, block_entry(0, n), block_entry(1, n))
            g32[n // 4, n % 4] = value
            s1[n // 4, n % 4] = value.astype(BF16)

    away = lax.rem(t + 2, 4)

    def sib_index(zz, ab, i):
        return (zz // 2 - zl) * (zz // 2 - zl) * 8 + ab * 4 + i

    def sibcopy(zz, ab, i):
        n = sib_index(zz, ab, i)
        return rcopy(pbuf.at[zz, ab, i], rbuf.at[n], ss.at[n], sr.at[n], sib)

    def qcopy(ab, i):
        return rcopy(pbuf.at[away, ab, i], qbuf.at[ab * 4 + i], qs.at[ab * 4 + i], qr.at[ab * 4 + i], zpair)

    def unit(zz, ab, i):
        w = (wa, wb)[ab][zz, i].reshape(256, 512)
        tile = ((ab * 4 + zz) * 4 + i) * 2
        left = jnp.concatenate([normed[tile], normed[tile + 1]], axis=1)
        acc[...] += jnp.dot(left, w, preferred_element_type=F32)
        both = jnp.concatenate([cot[j] for j in range(4)], axis=1)
        part = lax.dot_general(both, w, (((1,), (1,)), ((), ())), preferred_element_type=F32)
        pbuf[zz, ab, i] = part.astype(BF16)

        @pl.when(lax.rem(zz + t, 2) == 1)
        def _():
            sibcopy(zz, ab, i).start()

    def combine(zz, ab, i):
        @pl.when(lax.rem(zz + t, 2) == 0)
        def _():
            n = sib_index(zz, ab, i)
            rcopy(rbuf.at[n], rbuf.at[n], ss.at[n], sr.at[n], sib).wait_recv()
            pbuf[zz, ab, i] = (pbuf[zz, ab, i].astype(F32) + rbuf[n].astype(F32)).astype(BF16)

        @pl.when(zz == away)
        def _():
            qcopy(ab, i).start()

    waiting = []

    def units(zz, d):
        for ab, i in ((0, m4(y + d)), (1, m4(x + d))):
            unit(zz, ab, i)
            while waiting:
                combine(*waiting.pop())
            waiting.append((zz, ab, i))

    dist = (1, -1, 2)

    def bg_copy(stage, d, incoming):
        back = d if incoming else 0
        over_x = stage in (1, 2)
        sender = m4((x if over_x else y) - back)
        target = m4(sender + d)
        dev = xdev(d) if over_x else ydev(d)
        if stage == 0:
            src, dst = s1.at[target], r1.at[sender]
        elif stage == 1:
            src, dst = s2.at[target], r2.at[sender]
        else:
            src = dst = tall.at[y, sender] if over_x else tall.at[sender]
        i = stage * 3 + dist.index(d)
        return rcopy(src, dst, bs.at[i], br.at[i], dev)

    def bg_send(stage):
        for d in dist:
            c = bg_copy(stage, d, False)
            c.start()
            sent.append(c)

    def bg_recv(stage):
        for d in dist:
            bg_copy(stage, d, True).wait_recv()

    turn = 2 * zl - 1

    def ring(k, incoming):
        ref = gz.at[m4(zh - (k + incoming) * turn)]
        return rcopy(ref, ref, bs.at[12 + k], br.at[12 + k], {"fsdp": m4(zh + turn) * 4 + x})

    def ring_send(k):
        c = ring(k, 0)
        c.start()
        sent.append(c)

    def ring_step(k):
        ring(k, 1).wait_recv()
        if k < 2:
            ring_send(k + 1)
            return
        total = gz[0].astype(F32)
        for i in range(1, 4):
            total = total + gz[i].astype(F32)
        tall[y, x] = total.astype(BF16)
        bg_send(2)

    def bg_sum(stage):
        bg_recv(stage)
        if stage == 0:
            total = g32[y]
            for d in dist:
                total = total + r1[m4(y - d)].astype(F32)
            p1[...] = total
            s2[...] = total.astype(BF16)
            bg_send(1)
        else:
            total = p1[x]
            for d in dist:
                total = total + r2[m4(x - d)].astype(F32)
            gz[zh] = total.astype(BF16)
            ring_send(0)

    own_away = (zh // 2 - zl) * (zh // 2 - zl)
    step = 1 - 2 * (zh % 2)
    partner, near, far = m4(zh + step), m4(zh - step), m4(zh + 2)
    p0_, p1_ = zh, own_away * partner + (1 - own_away) * near
    p2_ = own_away * near + (1 - own_away) * far
    p3_ = own_away * far + (1 - own_away) * partner
    adjacent = own_away * near + (1 - own_away) * partner

    def small_a(zz):
        recv(zz, AXP)
        send(zz, AXFP)
        recv(zz, AXM)
        send(zz, AXFM)

    def small_b(zz):
        recv(zz, BYP)
        send(zz, BYFP)
        recv(zz, BYM)
        send(zz, BYFM)

    def big_first(zz):
        recv(zz, AXFP, AXFM)
        send(zz, AYP0, AYM1)
        recv(zz, BYFP, BYFM)
        send(zz, BXP0, BXM1)

    def big_second(zz):
        send(zz, AYP1, AYM0, BXP1, BXM0)

    def big_forward(zz):
        for got, kind in ((AYP0, AYFP), (BXP0, BXFP), (AYM1, AYFM), (BXM1, BXFM)):
            recv(zz, got)
            send(zz, kind)

    def big_middle(zz):
        recv(zz, AYP1, AYM0, BXP1, BXM0)

    def big_end(zz):
        recv(zz, AYFP, AYFM, BXFP, BXFM)

    for i in range(4):
        loads[i].wait()
    zsend(ZAP, ZAM, ZBP, ZBM)
    send(p0_, AXP, AXM, BYP, BYM)
    loads[4].wait()
    norm_rows(0)
    norm_rows(1)
    small_a(p0_)
    small_b(p0_)
    norm_rows(2)
    zrecv(ZAP, ZAM)
    zsend(ZFP)
    send(p1_, AXP, AXM)
    send(adjacent, AXP, AXM)
    norm_rows(3)
    big_first(p0_)
    zrecv(ZBP, ZBM)
    zsend(ZFM)
    send(p1_, BYP, BYM)
    send(adjacent, BYP, BYM)
    norm_rows(4)
    norm_rows(5)
    for i in range(5, first_rows):
        loads[i].wait()
    block_products(0, 5)
    small_a(p1_)
    small_b(p1_)
    block_products(5, 8)
    small_a(adjacent)
    small_b(adjacent)
    zrecv(ZFP, ZFM)
    send(far, AXP, AXM, BYP, BYM)
    acc[...] = jnp.zeros_like(acc)
    big_first(p1_)
    units(p1_, 0)
    units(p0_, 0)
    block_products(8, 11)
    small_a(far)
    small_b(far)
    big_second(p1_)
    block_products(11, 16)
    bg_send(0)
    big_first(p2_)
    units(p2_, 0)
    big_forward(p1_)
    big_second(p2_)
    bg_sum(0)
    big_middle(p1_)
    units(p1_, 1)
    units(p1_, -1)
    big_forward(p0_)
    big_second(p0_)
    big_end(p1_)
    units(p1_, 2)
    big_forward(p2_)
    big_first(p3_)
    bg_sum(1)
    big_middle(p2_)
    units(p2_, 1)
    units(p2_, -1)
    big_middle(p0_)
    units(p0_, 1)
    units(p0_, -1)
    ring_step(0)
    big_second(p3_)
    big_end(p0_)
    units(p0_, 2)
    ring_step(1)
    big_end(p2_)
    units(p2_, 2)
    big_forward(p3_)
    units(p3_, 0)
    ring_step(2)
    bg_recv(2)
    bg_send(3)
    big_middle(p3_)
    units(p3_, 1)
    units(p3_, -1)
    big_end(p3_)
    units(p3_, 2)
    combine(*waiting.pop())
    key_out[...] = acc[:, 0:256].astype(BF16)
    value_out[...] = acc[:, 256:512].astype(BF16)
    bg_recv(3)
    gall[...] = tall[...].astype(F32).reshape(1024, 128)
    low8 = lanes(8)
    for h in range(2):
        for k in range(32):
            even = gall[pl.ds(h * 512 + 2 * k, 8, stride=64), :]
            odd = gall[pl.ds(h * 512 + 2 * k + 1, 8, stride=64), :]
            rows, cols = pl.ds(h * 8, 8), pl.ds(k * 128, 128)
            bg_out[0, rows, cols] = jnp.where(low8, even, pltpu.roll(odd, 64, 1))
            bg_out[1, rows, cols] = jnp.where(low8, pltpu.roll(even, 64, 1), odd)

    for ab in range(2):
        for i in range(4):
            n = ab * 4 + i
            rcopy(qbuf.at[n], qbuf.at[n], qs.at[n], qr.at[n], zpair).wait_recv()

    @pl.loop(0, TOK // 16)
    def _(k):
        rows = pl.ds(pl.multiple_of(k * 16, 16), 16)
        low = lanes(16)

        def tile(ab, i, half):
            cols = pl.ds(half * 128, 128)
            n = ab * 4 + i
            return pbuf[t, ab, i, rows, cols].astype(F32) + qbuf[n, rows, cols].astype(F32)

        for hx in range(2):
            for hq in range(2):
                for b in range(2):
                    a_tile = tile(0, 2 * hq + b, hx)
                    a_tiles = (a_tile, pltpu.roll(a_tile, 64, 1))
                    for a in range(2):
                        b_tile = tile(1, 2 * hx + a, hq)
                        if b == 0:
                            b_tile = pltpu.roll(b_tile, 64, 1)
                        cols = pl.ds(((2 * hx + a) * 4 + 2 * hq + b) * 128, 128)
                        grad_out[rows, cols] = jnp.where(low, a_tiles[a], b_tile).astype(BF16)

    for c in sent:
        c.wait_send()
    for n in range(16):
        rcopy(pbuf.at[0, 0, 0], rbuf.at[n], ss.at[n], sr.at[n], sib).wait_send()
    for ab in range(2):
        for i in range(4):
            qcopy(ab, i).wait_send()


def write_out(*refs):
    copies = [pltpu.make_async_copy(refs[i], refs[4 + i], refs[8].at[i]) for i in range(4)]
    for c in copies:
        c.start()
    for c in copies:
        c.wait()


def local(activations, norm_gain, key_weight, value_weight, key_cot, value_cot, blocks):
    any_spec = pl.BlockSpec(memory_space=pl.ANY)
    vmem_spec = pl.BlockSpec(memory_space=pltpu.VMEM)
    dma = pltpu.SemaphoreType.DMA
    key_out, value_out, grad, bg = pl.pallas_call(
        body,
        out_shape=(
            pltpu.VMEM((TOK, 256), BF16),
            pltpu.VMEM((TOK, 256), BF16),
            pltpu.VMEM((TOK, 2048), BF16),
            pltpu.VMEM((2, 16, 4096), F32),
        ),
        in_specs=[any_spec] * 6 + [pl.BlockSpec(memory_space=pltpu.SMEM)],
        out_specs=(vmem_spec,) * 4,
        scratch_shapes=[
            pltpu.VMEM((4, 4, 4, 64, 512), BF16),
            pltpu.VMEM((4, 4, 4, 64, 512), BF16),
            pltpu.VMEM((TOK, D), BF16),
            pltpu.VMEM((D // 128, TOK, 128), BF16),
            pltpu.VMEM((1, D), F32),
            pltpu.VMEM((4, TOK, 128), BF16),
            pltpu.VMEM((TOK, 512), F32),
            pltpu.VMEM((4, 2, 4, TOK, 256), BF16),
            pltpu.VMEM((16, TOK, 256), BF16),
            pltpu.VMEM((8, TOK, 256), BF16),
            pltpu.VMEM((4, 4, 64, 128), F32),
            pltpu.VMEM((4, 4, 64, 128), BF16),
            pltpu.VMEM((4, 4, 64, 128), BF16),
            pltpu.VMEM((4, 64, 128), F32),
            pltpu.VMEM((4, 64, 128), BF16),
            pltpu.VMEM((4, 64, 128), BF16),
            pltpu.VMEM((4, 64, 128), BF16),
            pltpu.VMEM((4, 4, 64, 128), BF16),
            pltpu.VMEM((1024, 128), F32),
            dma((9 + TOK // ROWS,)),
            dma((20, 4)),
            dma((20, 4)),
            dma((6,)),
            dma((6,)),
            dma((15,)),
            dma((15,)),
            dma((16,)),
            dma((16,)),
            dma((8,)),
            dma((8,)),
        ],
        compiler_params=pltpu.CompilerParams(
            collective_id=0, has_side_effects=True, vmem_limit_bytes=60 * 1024 * 1024
        ),
        name="kv_step",
    )(
        activations,
        norm_gain.reshape(1, D),
        key_weight.reshape(4, 2, 64, 256),
        value_weight.reshape(4, 2, 64, 256),
        key_cot,
        value_cot,
        blocks.transpose(0, 2, 1),
    )
    results = (key_out, value_out, grad, bg)
    return pl.pallas_call(
        write_out,
        out_shape=tuple(jax.ShapeDtypeStruct(r.shape, r.dtype) for r in results),
        in_specs=[any_spec] * 4,
        out_specs=(any_spec,) * 4,
        scratch_shapes=[dma((4,))],
        compiler_params=pltpu.CompilerParams(vmem_limit_bytes=1024 * 1024),
        name="write_out",
    )(*results)


def solution(mesh):
    in_specs = (
        P(("fsdp", "replica"), None),
        P(),
        P("fsdp", "tensor"),
        P("fsdp", "tensor"),
        P(("fsdp", "replica"), "tensor"),
        P(("fsdp", "replica"), "tensor"),
        P(None, "tensor", None),
    )
    out_specs = (
        P(("fsdp", "replica"), "tensor"),
        P(("fsdp", "replica"), "tensor"),
        P(("fsdp", "replica"), "tensor"),
        P(None, "tensor", None),
    )
    return jax.shard_map(local, mesh=mesh, in_specs=in_specs, out_specs=out_specs, check_vma=False)
```

```python
import functools

import jax
import jax.numpy as jnp
from jax import lax
from jax.experimental import pallas as pl
from jax.experimental.pallas import tpu as pltpu
from jax.sharding import PartitionSpec as P

D = 8192
TOK = 384
EPS = 1e-05
F32 = jnp.float32
BF16 = jnp.bfloat16
ROWS = 64

AXP, AXM, AXFP, AXFM, BYP, BYM, BYFP, BYFM = range(8)
AYP0, AYP1, AYM0, AYM1, AYFP, AYFM, BXP0, BXP1, BXM0, BXM1, BXFP, BXFM = range(8, 20)
ZAP, ZAM, ZBP, ZBM, ZFP, ZFM = range(6)


def body(
    act_hbm, gain_hbm, kw_hbm, vw_hbm, kc_hbm, vc_hbm, blocks,
    key_out, value_out, grad_out, bg_out,
    wa, wb, act, normed, gain, cot, acc, pbuf, rbuf, qbuf,
    g32, s1, r1, p1, s2, r2, gz, tall, gall,
    ld, xs, xr, zs, zr, bs, br, ss, sr, qs, qr,
):
    f = lax.axis_index("fsdp")
    t = lax.axis_index("tensor")
    y = lax.axis_index("replica")
    zh, x = f // 4, f % 4
    zl = t // 2

    def m4(v):
        return lax.rem(v + 4, 4)

    def xdev(d):
        return {"fsdp": zh * 4 + m4(x + d)}

    def ydev(d):
        return {"replica": m4(y + d)}

    def zdev(d):
        return {"fsdp": m4(zh + d) * 4 + x}

    sib = {"tensor": t + 1 - 2 * (t % 2)}
    zpair = {"tensor": lax.rem(t + 2, 4)}

    loads = []

    def load(src, dst):
        c = pltpu.make_async_copy(src, dst, ld.at[len(loads)])
        c.start()
        loads.append(c)

    for i, w_hbm in enumerate((kw_hbm, vw_hbm)):
        load(w_hbm.at[y, 0], wa.at[zh, y, x, :, pl.ds(i * 256, 256)])
        load(w_hbm.at[y, 1], wb.at[zh, x, y, :, pl.ds(i * 256, 256)])
    load(gain_hbm, gain)
    for i in range(4):
        load((kc_hbm, vc_hbm)[i // 2].at[:, pl.ds(i % 2 * 128, 128)], cot.at[i])
    first_rows = len(loads)
    for i in range(TOK // ROWS):
        load(act_hbm.at[pl.ds(i * ROWS, ROWS)], act.at[pl.ds(i * ROWS, ROWS)])

    barrier = pltpu.get_barrier_semaphore()
    peers = [xdev(1), xdev(-1), xdev(2), ydev(1), ydev(-1), ydev(2), zdev(1), zdev(-1), sib, zpair]
    for peer in peers:
        pl.semaphore_signal(barrier, inc=1, device_id=peer, device_id_type=pl.DeviceIdType.MESH)
    pl.semaphore_wait(barrier, len(peers))

    sent = []

    def rcopy(src, dst, a, b, dev):
        return pltpu.make_async_remote_copy(
            src_ref=src, dst_ref=dst, send_sem=a, recv_sem=b, device_id=dev,
            device_id_type=pl.DeviceIdType.MESH,
        )

    def piece(kind, zz, px, py):
        if kind in (AXP, AXM):
            return wa.at[zz, py, px]
        if kind == AXFP:
            return wa.at[zz, py, m4(px - 1), pl.ds(0, 32)]
        if kind == AXFM:
            return wa.at[zz, py, m4(px + 1), pl.ds(32, 32)]
        if kind in (BYP, BYM):
            return wb.at[zz, px, py]
        if kind == BYFP:
            return wb.at[zz, px, m4(py - 1), pl.ds(0, 32)]
        if kind == BYFM:
            return wb.at[zz, px, m4(py + 1), pl.ds(32, 32)]
        if kind in (AYP0, AYM0):
            return wa.at[zz, py, pl.ds(0, 2)]
        if kind in (AYP1, AYM1):
            return wa.at[zz, py, pl.ds(2, 2)]
        if kind == AYFP:
            return wa.at[zz, m4(py - 1), pl.ds(0, 2)]
        if kind == AYFM:
            return wa.at[zz, m4(py + 1), pl.ds(2, 2)]
        if kind in (BXP0, BXM0):
            return wb.at[zz, px, pl.ds(0, 2)]
        if kind in (BXP1, BXM1):
            return wb.at[zz, px, pl.ds(2, 2)]
        if kind == BXFP:
            return wb.at[zz, m4(px - 1), pl.ds(0, 2)]
        return wb.at[zz, m4(px + 1), pl.ds(2, 2)]

    along_x = (AXP, AXM, AXFP, AXFM, BXP0, BXP1, BXM0, BXM1, BXFP, BXFM)
    plus = (AXP, AXFP, BYP, BYFP, AYP0, AYP1, AYFP, BXP0, BXP1, BXFP)

    def xy(kind, zz, incoming):
        d = 1 if kind in plus else -1
        back = d if incoming else 0
        if kind in along_x:
            ref, dev = piece(kind, zz, m4(x - back), y), xdev(d)
        else:
            ref, dev = piece(kind, zz, x, m4(y - back)), ydev(d)
        return rcopy(ref, ref, xs.at[kind, zz], xr.at[kind, zz], dev)

    def send(zz, *kinds):
        for kind in kinds:
            c = xy(kind, zz, False)
            c.start()
            sent.append(c)

    def recv(zz, *kinds):
        for kind in kinds:
            xy(kind, zz, True).wait_recv()

    def along_z(kind, incoming):
        d = 1 if kind in (ZAP, ZBP, ZFP) else -1
        pz = m4(zh - d) if incoming else zh
        if kind in (ZAP, ZAM):
            ref = wa.at[pz, y, x]
        elif kind in (ZBP, ZBM):
            ref = wb.at[pz, x, y]
        elif kind == ZFP:
            ref = wa.at[m4(pz - 1), y, x]
        else:
            ref = wb.at[m4(pz + 1), x, y]
        return rcopy(ref, ref, zs.at[kind], zr.at[kind], zdev(d))

    def zsend(*kinds):
        for kind in kinds:
            c = along_z(kind, False)
            c.start()
            sent.append(c)

    def zrecv(*kinds):
        for kind in kinds:
            along_z(kind, True).wait_recv()

    def lanes(rows):
        return lax.broadcasted_iota(jnp.int32, (rows, 128), 1) < 64

    def norm_rows(i):
        loads[first_rows + i].wait()
        low = lanes(16)

        @pl.loop(0, ROWS // 16)
        def _(k):
            rows = pl.ds(pl.multiple_of(i * ROWS + k * 16, 16), 16)
            total = jnp.zeros((16, 128), F32)
            for j in range(D // 512):
                v = act[rows, pl.ds(j * 512, 512)].astype(F32)
                v = v * v
                total = total + ((v[:, 0:128] + v[:, 128:256]) + (v[:, 256:384] + v[:, 384:512]))
            inv = lax.rsqrt(jnp.sum(total, axis=1, keepdims=True) / D + EPS)

            def tile(zz, xx, q):
                cols = pl.ds((zz * 16 + xx * 4 + q) * 128, 128)
                return act[rows, cols].astype(F32) * inv * gain[:, cols]

            for zz in range(4):
                for hx in range(2):
                    for hq in range(2):
                        ee, eo = tile(zz, 2 * hx, 2 * hq), tile(zz, 2 * hx, 2 * hq + 1)
                        oe, oo = tile(zz, 2 * hx + 1, 2 * hq), tile(zz, 2 * hx + 1, 2 * hq + 1)
                        ree, roe, roo = pltpu.roll(ee, 64, 1), pltpu.roll(oe, 64, 1), pltpu.roll(oo, 64, 1)
                        a0, b0 = (zz * 4 + 2 * hq) * 2 + hx, ((4 + zz) * 4 + 2 * hx) * 2 + hq
                        normed[a0, rows] = jnp.where(low, ee, roe).astype(BF16)
                        normed[a0 + 2, rows] = jnp.where(low, eo, roo).astype(BF16)
                        normed[b0, rows] = jnp.where(low, ree, eo).astype(BF16)
                        normed[b0 + 2, rows] = jnp.where(low, roe, oo).astype(BF16)

    def block_entry(p, n):
        row, column = blocks[p, 0, n], blocks[p, 1, n]
        zz, xx, q, odd = lax.div(row, 32), lax.rem(lax.div(row, 8), 4), lax.rem(lax.div(row, 2), 4), lax.rem(row, 2)
        in_a = zz * 8 + q * 2 + lax.div(xx, 2)
        in_b = 32 + zz * 8 + xx * 2 + lax.div(q, 2)
        left = normed[in_a * (1 - odd) + in_b * odd]
        half = lax.rem(xx, 2) * (1 - odd) + lax.rem(q, 2) * odd
        right = cot[2 * p + lax.div(column, 2)]
        full = lax.dot_general(left, right, (((0,), (0,)), ((), ())), preferred_element_type=F32)
        low = half.astype(F32)
        half = full[64:] * low + full[:64] * (1.0 - low)
        column_odd = lax.rem(column, 2).astype(F32)
        move = column_odd if p == 0 else 1.0 - column_odd
        return pltpu.roll(half, 64, 1) * move + half * (1.0 - move)

    def block_products(lo, hi):
        low = lanes(64)

        @pl.loop(lo, hi)
        def _(n):
            value = jnp.where(low, block_entry(0, n), block_entry(1, n))
            g32[n // 4, n % 4] = value
            s1[n // 4, n % 4] = value.astype(BF16)

    away = lax.rem(t + 2, 4)

    def sib_index(zz, ab, i):
        return (zz // 2 - zl) * (zz // 2 - zl) * 8 + ab * 4 + i

    def sibcopy(zz, ab, i):
        n = sib_index(zz, ab, i)
        return rcopy(pbuf.at[zz, ab, i], rbuf.at[n], ss.at[n], sr.at[n], sib)

    def qcopy(ab, i):
        return rcopy(pbuf.at[away, ab, i], qbuf.at[ab * 4 + i], qs.at[ab * 4 + i], qr.at[ab * 4 + i], zpair)

    def unit(zz, ab, i):
        w = (wa, wb)[ab][zz, i].reshape(256, 512)
        tile = ((ab * 4 + zz) * 4 + i) * 2
        left = jnp.concatenate([normed[tile], normed[tile + 1]], axis=1)
        acc[...] += jnp.dot(left, w, preferred_element_type=F32)
        both = jnp.concatenate([cot[j] for j in range(4)], axis=1)
        part = lax.dot_general(both, w, (((1,), (1,)), ((), ())), preferred_element_type=F32)
        pbuf[zz, ab, i] = part.astype(BF16)

        @pl.when(lax.rem(zz + t, 2) == 1)
        def _():
            sibcopy(zz, ab, i).start()

    def combine(zz, ab, i):
        @pl.when(lax.rem(zz + t, 2) == 0)
        def _():
            n = sib_index(zz, ab, i)
            rcopy(rbuf.at[n], rbuf.at[n], ss.at[n], sr.at[n], sib).wait_recv()
            pbuf[zz, ab, i] = (pbuf[zz, ab, i].astype(F32) + rbuf[n].astype(F32)).astype(BF16)

        @pl.when(zz == away)
        def _():
            qcopy(ab, i).start()

    waiting = []

    def units(zz, d):
        for ab, i in ((0, m4(y + d)), (1, m4(x + d))):
            unit(zz, ab, i)
            while waiting:
                combine(*waiting.pop())
            waiting.append((zz, ab, i))

    dist = (1, -1, 2)

    def bg_copy(stage, d, incoming):
        back = d if incoming else 0
        over_x = stage in (1, 3)
        sender = m4((x if over_x else y) - back)
        target = m4(sender + d)
        dev = xdev(d) if over_x else ydev(d)
        if stage == 0:
            src, dst = s1.at[target], r1.at[sender]
        elif stage == 1:
            src, dst = s2.at[target], r2.at[sender]
        else:
            src = dst = tall.at[sender] if over_x else tall.at[x, sender]
        i = stage * 3 + dist.index(d)
        return rcopy(src, dst, bs.at[i], br.at[i], dev)

    def bg_send(stage):
        for d in dist:
            c = bg_copy(stage, d, False)
            c.start()
            sent.append(c)

    def bg_recv(stage):
        for d in dist:
            bg_copy(stage, d, True).wait_recv()

    turn = 2 * zl - 1

    def ring(k, incoming):
        ref = gz.at[m4(zh - (k + incoming) * turn)]
        return rcopy(ref, ref, bs.at[12 + k], br.at[12 + k], {"fsdp": m4(zh + turn) * 4 + x})

    def ring_send(k):
        c = ring(k, 0)
        c.start()
        sent.append(c)

    def ring_step(k):
        ring(k, 1).wait_recv()
        if k < 2:
            ring_send(k + 1)
            return
        total = gz[0].astype(F32)
        for i in range(1, 4):
            total = total + gz[i].astype(F32)
        tall[x, y] = total.astype(BF16)
        bg_send(2)

    def bg_sum(stage):
        bg_recv(stage)
        if stage == 0:
            total = g32[y]
            for d in dist:
                total = total + r1[m4(y - d)].astype(F32)
            p1[...] = total
            s2[...] = total.astype(BF16)
            bg_send(1)
        else:
            total = p1[x]
            for d in dist:
                total = total + r2[m4(x - d)].astype(F32)
            gz[zh] = total.astype(BF16)
            ring_send(0)

    own_away = (zh // 2 - zl) * (zh // 2 - zl)
    step = 1 - 2 * (zh % 2)
    partner, near, far = m4(zh + step), m4(zh - step), m4(zh + 2)
    p0_, p1_ = zh, own_away * partner + (1 - own_away) * near
    p2_ = own_away * near + (1 - own_away) * far
    p3_ = own_away * far + (1 - own_away) * partner
    adjacent = own_away * near + (1 - own_away) * partner

    def small_a(zz):
        recv(zz, AXP)
        send(zz, AXFP)
        recv(zz, AXM)
        send(zz, AXFM)

    def small_b(zz):
        recv(zz, BYP)
        send(zz, BYFP)
        recv(zz, BYM)
        send(zz, BYFM)

    def big_first(zz):
        recv(zz, AXFP, AXFM)
        send(zz, AYP0, AYM1)
        recv(zz, BYFP, BYFM)
        send(zz, BXP0, BXM1)

    def big_second(zz):
        send(zz, AYP1, AYM0, BXP1, BXM0)

    def big_forward(zz):
        for got, kind in ((AYP0, AYFP), (BXP0, BXFP), (AYM1, AYFM), (BXM1, BXFM)):
            recv(zz, got)
            send(zz, kind)

    def big_middle(zz):
        recv(zz, AYP1, AYM0, BXP1, BXM0)

    def big_end(zz):
        recv(zz, AYFP, AYFM, BXFP, BXFM)

    for i in range(4):
        loads[i].wait()
    zsend(ZAP, ZAM, ZBP, ZBM)
    send(p0_, AXP, AXM, BYP, BYM)
    loads[4].wait()
    norm_rows(0)
    norm_rows(1)
    small_a(p0_)
    small_b(p0_)
    norm_rows(2)
    zrecv(ZAP, ZAM)
    zsend(ZFP)
    send(p1_, AXP, AXM)
    send(adjacent, AXP, AXM)
    norm_rows(3)
    big_first(p0_)
    zrecv(ZBP, ZBM)
    zsend(ZFM)
    send(p1_, BYP, BYM)
    send(adjacent, BYP, BYM)
    norm_rows(4)
    norm_rows(5)
    for i in range(5, first_rows):
        loads[i].wait()
    block_products(0, 5)
    small_a(p1_)
    small_b(p1_)
    block_products(5, 8)
    small_a(adjacent)
    small_b(adjacent)
    zrecv(ZFP, ZFM)
    send(far, AXP, AXM, BYP, BYM)
    acc[...] = jnp.zeros_like(acc)
    big_first(p1_)
    units(p1_, 0)
    units(p0_, 0)
    block_products(8, 11)
    small_a(far)
    small_b(far)
    big_second(p1_)
    block_products(11, 16)
    bg_send(0)
    big_first(p2_)
    units(p2_, 0)
    big_forward(p1_)
    big_second(p2_)
    bg_sum(0)
    big_middle(p1_)
    units(p1_, 1)
    units(p1_, -1)
    big_forward(p0_)
    big_second(p0_)
    big_end(p1_)
    units(p1_, 2)
    big_forward(p2_)
    big_first(p3_)
    bg_sum(1)
    big_middle(p2_)
    units(p2_, 1)
    units(p2_, -1)
    big_middle(p0_)
    units(p0_, 1)
    units(p0_, -1)
    ring_step(0)
    big_second(p3_)
    big_end(p0_)
    units(p0_, 2)
    ring_step(1)
    big_end(p2_)
    units(p2_, 2)
    big_forward(p3_)
    units(p3_, 0)
    ring_step(2)
    bg_recv(2)
    bg_send(3)
    big_middle(p3_)
    units(p3_, 1)
    units(p3_, -1)
    big_end(p3_)
    units(p3_, 2)
    combine(*waiting.pop())
    key_out[...] = acc[:, 0:256].astype(BF16)
    value_out[...] = acc[:, 256:512].astype(BF16)
    bg_recv(3)
    for i in range(16):
        gall[pl.ds(i * 64, 64), :] = tall[i % 4, i // 4].astype(F32)
    low8 = lanes(8)
    for h in range(2):
        for k in range(32):
            even = gall[pl.ds(h * 512 + 2 * k, 8, stride=64), :]
            odd = gall[pl.ds(h * 512 + 2 * k + 1, 8, stride=64), :]
            rows, cols = pl.ds(h * 8, 8), pl.ds(k * 128, 128)
            bg_out[0, rows, cols] = jnp.where(low8, even, pltpu.roll(odd, 64, 1))
            bg_out[1, rows, cols] = jnp.where(low8, pltpu.roll(even, 64, 1), odd)

    for ab in range(2):
        for i in range(4):
            n = ab * 4 + i
            rcopy(qbuf.at[n], qbuf.at[n], qs.at[n], qr.at[n], zpair).wait_recv()

    @pl.loop(0, TOK // 16)
    def _(k):
        rows = pl.ds(pl.multiple_of(k * 16, 16), 16)
        low = lanes(16)

        def tile(ab, i, half):
            cols = pl.ds(half * 128, 128)
            n = ab * 4 + i
            return pbuf[t, ab, i, rows, cols].astype(F32) + qbuf[n, rows, cols].astype(F32)

        for hx in range(2):
            for hq in range(2):
                for b in range(2):
                    a_tile = tile(0, 2 * hq + b, hx)
                    a_tiles = (a_tile, pltpu.roll(a_tile, 64, 1))
                    for a in range(2):
                        b_tile = tile(1, 2 * hx + a, hq)
                        if b == 0:
                            b_tile = pltpu.roll(b_tile, 64, 1)
                        cols = pl.ds(((2 * hx + a) * 4 + 2 * hq + b) * 128, 128)
                        grad_out[rows, cols] = jnp.where(low, a_tiles[a], b_tile).astype(BF16)

    for c in sent:
        c.wait_send()
    for n in range(16):
        rcopy(pbuf.at[0, 0, 0], rbuf.at[n], ss.at[n], sr.at[n], sib).wait_send()
    for ab in range(2):
        for i in range(4):
            qcopy(ab, i).wait_send()


def write_out(*refs):
    copies = [pltpu.make_async_copy(refs[i], refs[4 + i], refs[8].at[i]) for i in range(4)]
    for c in copies:
        c.start()
    for c in copies:
        c.wait()


def local(activations, norm_gain, key_weight, value_weight, key_cot, value_cot, blocks):
    any_spec = pl.BlockSpec(memory_space=pl.ANY)
    vmem_spec = pl.BlockSpec(memory_space=pltpu.VMEM)
    dma = pltpu.SemaphoreType.DMA
    key_out, value_out, grad, bg = pl.pallas_call(
        body,
        out_shape=(
            pltpu.VMEM((TOK, 256), BF16),
            pltpu.VMEM((TOK, 256), BF16),
            pltpu.VMEM((TOK, 2048), BF16),
            pltpu.VMEM((2, 16, 4096), F32),
        ),
        in_specs=[any_spec] * 6 + [pl.BlockSpec(memory_space=pltpu.SMEM)],
        out_specs=(vmem_spec,) * 4,
        scratch_shapes=[
            pltpu.VMEM((4, 4, 4, 64, 512), BF16),
            pltpu.VMEM((4, 4, 4, 64, 512), BF16),
            pltpu.VMEM((TOK, D), BF16),
            pltpu.VMEM((D // 128, TOK, 128), BF16),
            pltpu.VMEM((1, D), F32),
            pltpu.VMEM((4, TOK, 128), BF16),
            pltpu.VMEM((TOK, 512), F32),
            pltpu.VMEM((4, 2, 4, TOK, 256), BF16),
            pltpu.VMEM((16, TOK, 256), BF16),
            pltpu.VMEM((8, TOK, 256), BF16),
            pltpu.VMEM((4, 4, 64, 128), F32),
            pltpu.VMEM((4, 4, 64, 128), BF16),
            pltpu.VMEM((4, 4, 64, 128), BF16),
            pltpu.VMEM((4, 64, 128), F32),
            pltpu.VMEM((4, 64, 128), BF16),
            pltpu.VMEM((4, 64, 128), BF16),
            pltpu.VMEM((4, 64, 128), BF16),
            pltpu.VMEM((4, 4, 64, 128), BF16),
            pltpu.VMEM((1024, 128), F32),
            dma((9 + TOK // ROWS,)),
            dma((20, 4)),
            dma((20, 4)),
            dma((6,)),
            dma((6,)),
            dma((15,)),
            dma((15,)),
            dma((16,)),
            dma((16,)),
            dma((8,)),
            dma((8,)),
        ],
        compiler_params=pltpu.CompilerParams(
            collective_id=0, has_side_effects=True, vmem_limit_bytes=60 * 1024 * 1024
        ),
        name="kv_step",
    )(
        activations,
        norm_gain.reshape(1, D),
        key_weight.reshape(4, 2, 64, 256),
        value_weight.reshape(4, 2, 64, 256),
        key_cot,
        value_cot,
        blocks.transpose(0, 2, 1),
    )
    results = (key_out, value_out, grad, bg)
    return pl.pallas_call(
        write_out,
        out_shape=tuple(jax.ShapeDtypeStruct(r.shape, r.dtype) for r in results),
        in_specs=[any_spec] * 4,
        out_specs=(any_spec,) * 4,
        scratch_shapes=[dma((4,))],
        compiler_params=pltpu.CompilerParams(vmem_limit_bytes=1024 * 1024),
        name="write_out",
    )(*results)


def solution(mesh):
    in_specs = (
        P(("fsdp", "replica"), None),
        P(),
        P("fsdp", "tensor"),
        P("fsdp", "tensor"),
        P(("fsdp", "replica"), "tensor"),
        P(("fsdp", "replica"), "tensor"),
        P(None, "tensor", None),
    )
    out_specs = (
        P(("fsdp", "replica"), "tensor"),
        P(("fsdp", "replica"), "tensor"),
        P(("fsdp", "replica"), "tensor"),
        P(None, "tensor", None),
    )
    return jax.shard_map(local, mesh=mesh, in_specs=in_specs, out_specs=out_specs, check_vma=False)
```
